256 devices in a mesh: chain: 8 (over z), rows: 32 (over y, x, core).
Axes of the slice: x: 4, y: 4, z: 8, core: 2. Of those that a mesh axis runs over, the one named last changes fastest.
Arguments:
- right_side: bfloat16 [16384, 768], P(('chain', 'rows')), may hold values from -6 to 6
- entering: float32 [16384, 256], P(('chain', 'rows')), may hold values from -6 to 6
- first_updates: float32 [2048, 512], P('rows'), may hold values from -6 to 6
- diag_inverse: bfloat16 [8, 2048, 2048], P('chain', 'rows'), may hold values from -2 to 2, as said below
- tile_blocks: bfloat16 [8, 32, 128, 2048], P('chain', 'rows'), may hold values from -0.09375 to 0.09375
- target_row_blocks: int32 [8, 32], P('chain', 'rows'), may hold values from 0 to 15
- tile_usage_order: int32 [8, 32], P('chain'), may hold values from 0 to 31, each once within a row
- live_tile_count: int32 [8], P('chain'), may hold values from 8 to 32
Outputs:
- solution: float32 [16384, 768], P(('chain', 'rows'))
- updates: float32 [16384, 768], P(('chain', 'rows'))
The draws below stay inside these ranges and needn't reach their ends.
Inputs may be any that keep to these rules, and one draw needn't show every extreme that they name: `diag_inverse`: lower triangular. `tile_usage_order`: each row names each of the 32 slots once; the first live_tile_count[s] entries name the live slots of supernode s.
All inputs are finite; a program needn't handle non-finite values.
Results may differ from the reference program's by a relative error of at most 0.013.
Values may be sent and summed in bfloat16 or wider, within the bound.
A program may use at most 64 MiB of HBM per device.

```python
import math
import jax
import jax.numpy as jnp
from jax import lax

W = 2048
TILE = 128
PW = 256
TICKS = 3
TPD = 1
NS = 8
TT = 32
NB = 16
ORDER = 16384
N_ROWS = 32


def draw_diag_inverse(key, part):
    first_key, second_key = jax.random.split(jax.random.fold_in(key, 17))
    scales = jax.random.uniform(first_key, (NS, W, 1), jnp.float32, 0.5, 1.5)
    lower = jax.random.normal(second_key, (NS, W, W), jnp.float32) * (0.8 / math.sqrt(W))
    row_index = lax.broadcasted_iota(jnp.int32, (W, W), 0)
    col_index = lax.broadcasted_iota(jnp.int32, (W, W), 1)
    below = (col_index < row_index).astype(jnp.float32)
    diagonal_mask = (col_index == row_index).astype(jnp.float32)
    return (lower * below[None] + scales * diagonal_mask[None]).astype(jnp.bfloat16)


def place_ends(values, stream_key, smallest, top_value):
    longest = values.shape.index(max(values.shape))
    spots = []
    for shift in (0, 1):
        where = [jax.random.randint(jax.random.fold_in(stream_key, axis), (), 0, length) for axis, length in enumerate(values.shape)]
        where[longest] = (where[longest] + shift) % values.shape[longest]
        spots.append(tuple(where))
    return values.at[spots[0]].set(smallest).at[spots[1]].set(top_value)


def steps_of(own_key, dims, cuts, smallest, top_value):
    factor_of = 1.0
    for dim, blocks in cuts:
        steps = jax.random.uniform(jax.random.fold_in(jax.random.fold_in(own_key, 6), dim), (blocks,), jnp.float32, smallest / len(cuts), top_value / len(cuts))
        factor_of = factor_of * jnp.repeat(jnp.exp(steps), dims[dim] // blocks).reshape((-1,) + (1,) * (len(dims) - 1 - dim))
    return factor_of


def noise(key, dims, width, limit, cuts=(), kind=jnp.bfloat16):
    level = steps_of(key, dims, cuts, -0.22, 0.18) if cuts else 1.0
    drawn = jax.random.normal(key, dims, jnp.float32) * width * level
    return jnp.minimum(jnp.maximum(drawn, -limit), limit).astype(kind)


def setup_inputs(seed: int = 0) -> dict:
    key_of = jax.random.split(jax.random.key(seed), 9)
    return {
        "right_side": noise(key_of[0], (ORDER, TICKS * PW), 1.0, 6.0, ((0, 256),)),
        "entering": noise(key_of[1], (ORDER, PW), 1.0, 6.0, ((0, 256),), jnp.float32),
        "first_updates": noise(key_of[2], (W, (TICKS - 1) * PW), 1.0, 6.0, ((0, 32),), jnp.float32),
        "diag_inverse": draw_diag_inverse(jax.random.fold_in(key_of[8], 71), 0),
        "tile_blocks": noise(key_of[4], (NS, TT, TILE, W), (W * TT // NB) ** -0.5, 0.09375, ((0, 8), (1, 32))),
        "target_row_blocks": place_ends(jax.random.randint(key_of[5], (NS, TT), 0, NB), jax.random.fold_in(key_of[5], 1), 0, NB - 1).astype(jnp.int32),
        "tile_usage_order": jax.vmap(lambda own: jax.random.permutation(own, TT))(jax.random.split(key_of[6], NS)).reshape((NS, TT)).astype(jnp.int32),
        "live_tile_count": place_ends(jax.random.randint(key_of[7], (NS,), TT // 4, TT + 1), jax.random.fold_in(key_of[7], 1), TT // 4, TT).astype(jnp.int32),
    }


def supernode_work(head_rows, inverse_block, tiles, targets, order_row, live_count):
    every_slot = order_row.shape[0]
    positions = jnp.arange(every_slot, dtype=jnp.int32)
    block_index = jnp.arange(NB, dtype=jnp.int32)
    solved = jnp.dot(inverse_block, head_rows, preferred_element_type=jnp.float32)
    counted = positions < live_count
    matches = jnp.logical_and(order_row[None, :] == positions[:, None], counted[None, :])
    alive = jnp.sum(matches.astype(jnp.float32), axis=1)
    placing = (block_index[:, None] == targets[None, :]).astype(jnp.float32) * alive[None, :]
    device_tiles = tiles.reshape(N_ROWS, TPD, TILE, W)
    device_placing = jnp.transpose(placing.reshape(NB, N_ROWS, TPD), (1, 0, 2))
    head_wide = head_rows.astype(jnp.float32)

    def add_device(running, members):
        own_tiles, own_placing = members
        products = jnp.einsum("mtw,wp->mtp", own_tiles.astype(jnp.float32), head_wide, precision=lax.Precision.HIGHEST)
        partial_value = jnp.einsum("bm,mtp->btp", own_placing, products, precision=lax.Precision.HIGHEST).reshape(W, -1)
        rounded = lax.optimization_barrier(partial_value.astype(jnp.bfloat16))
        return running + rounded.astype(jnp.float32), None

    starting = jnp.zeros((W, head_rows.shape[1]), jnp.float32)
    handed, _ = lax.scan(add_device, starting, (device_tiles, device_placing))
    return solved, handed


def reference(right_side, entering, first_updates, diag_inverse, tile_blocks, target_row_blocks, tile_usage_order, live_tile_count):
    solved_cols = [[] for s in range(NS)]
    handed_cols = [[] for s in range(NS)]
    for tick in range(TICKS):
        for supernode in range(NS):
            if tick == 0:
                incoming = entering[supernode * W:(supernode + 1) * W]
            elif supernode == 0:
                incoming = first_updates[:, (tick - 1) * PW:tick * PW]
            else:
                incoming = handed_cols[supernode - 1][tick - 1]
            given_rows = right_side[supernode * W:(supernode + 1) * W, tick * PW:(tick + 1) * PW]
            head_rows = (given_rows.astype(jnp.float32) - incoming).astype(jnp.bfloat16)
            solved, handed = supernode_work(head_rows, diag_inverse[supernode], tile_blocks[supernode], target_row_blocks[supernode], tile_usage_order[supernode], live_tile_count[supernode])
            solved_cols[supernode].append(solved)
            handed_cols[supernode].append(handed)
    solution = jnp.concatenate([jnp.concatenate(solved_cols[s], axis=1) for s in range(NS)], axis=0)
    updates = jnp.concatenate([jnp.concatenate(handed_cols[s], axis=1) for s in range(NS)], axis=0)
    return solution, updates
```

```python
import jax
import jax.numpy as jnp
from jax import lax
from jax.experimental import pallas as pl
from jax.experimental.pallas import tpu as pltpu
from jax.sharding import PartitionSpec as P

PW = 256
TILE = 128
HALF = 64
W = 2048
NZ = 8
SIDE = 4
CHIPS = SIDE * SIDE
TICKS = 3
LANES = 128
F32 = jnp.float32
BF16 = jnp.bfloat16
MESH = pl.DeviceIdType.MESH
RING = (0, 1, 3, 2)
HOPS = (1, 3, 2)
SPREAD = tuple((a, b) for a in range(SIDE) for b in range(SIDE) if (a, b) != (0, 0))


def kernel(
    right_side, entering, first_updates, diag_inverse, tile_blocks, targets, order, count,
    sol_out, upd_out,
    given, enter, first, weights, blocks, placed, base, other_base, products, own_products,
    code_own, code_sib, code_send, codes, sol_send, sol_recv, back_send, back_recv,
    block_send, block_recv, last_send, last_recv,
    load_sem, sib_send, sib_recv, base_send, base_recv, code_s1, code_r1, code_s2, code_r2,
    ring_s1, ring_r1, ring_s2, ring_r2, back_s, back_r, red_s, red_r,
):
    s = lax.axis_index("chain")
    row = lax.axis_index("rows")
    core = lax.rem(row, 2)
    chip = row // 2
    x = lax.rem(chip, SIDE)
    y = chip // SIDE
    p1 = x + core * (y - x)
    p2 = y + core * (x - y)
    stride1 = 1 + 3 * core
    stride2 = 4 - 3 * core
    up = lax.rem(s + 1, NZ)
    down = lax.rem(s + NZ - 1, NZ)
    sibling = (s, row + 1 - 2 * core)

    def chip_at(d1, d2):
        return lax.rem(p1 + d1, SIDE) * stride1 + lax.rem(p2 + d2, SIDE) * stride2

    def at(plane, d1, d2):
        return (plane, chip_at(d1, d2) * 2 + core)

    def send(src, dst, ssem, rsem, device):
        copy = pltpu.make_async_remote_copy(
            src_ref=src, dst_ref=dst, send_sem=ssem, recv_sem=rsem,
            device_id=device, device_id_type=MESH,
        )
        copy.start()
        return copy

    barrier = pltpu.get_barrier_semaphore()
    partners = [sibling] + [at(s, a, b) for a, b in SPREAD]
    partners += [at(up, d, 0) for d in range(SIDE)] + [at(down, (SIDE - d) % SIDE, 0) for d in range(SIDE)]
    partners += [(up, row + 1 - 2 * core), (down, row + 1 - 2 * core)]
    for device in partners:
        pl.semaphore_signal(barrier, inc=1, device_id=device, device_id_type=MESH)

    my_rows = pl.ds(pl.multiple_of(core * HALF, HALF), HALF)
    tile_rows = pl.ds(pl.multiple_of(core * TILE, TILE), TILE)
    diag_rows = pl.ds(pl.multiple_of(2 * TILE + core * HALF, HALF), HALF)
    loads = [
        pltpu.make_async_copy(right_side, given, load_sem.at[0]),
        pltpu.make_async_copy(entering, enter, load_sem.at[1]),
        pltpu.make_async_copy(first_updates, first, load_sem.at[2]),
        pltpu.make_async_copy(tile_blocks.at[0, 0], weights.at[tile_rows], load_sem.at[3]),
        pltpu.make_async_copy(diag_inverse.at[0], weights.at[diag_rows], load_sem.at[4]),
    ]
    for copy in loads:
        copy.start()

    live = jnp.int32(0)
    for k in range(order.shape[1]):
        hit = jnp.logical_and(order[0, k] == row, k < count[0])
        live = live + hit.astype(jnp.int32)
    code = targets[0, 0] + CHIPS * (1 - live)
    code_rows = lax.broadcasted_iota(jnp.int32, (8, LANES), 0)
    code_own[...] = jnp.where(code_rows == core, code, 0)

    for copy in loads[:3]:
        copy.wait()
    is_first = (s == 0).astype(F32)

    def head_part(tick, half):
        lanes = pl.ds(pl.multiple_of(tick * PW + half * LANES, LANES), LANES)
        value = given[:, lanes].astype(F32)
        if tick == 0:
            taken = enter[:, pl.ds(pl.multiple_of(half * LANES, LANES), LANES)]
        else:
            lanes = pl.ds(pl.multiple_of((tick - 1) * PW + half * LANES, LANES), LANES)
            taken = is_first * first[:, lanes]
        return (value - taken).astype(BF16)

    for tick in range(TICKS):
        other_base[tick] = head_part(tick, 1 - core)
        base[tick, chip, my_rows] = head_part(tick, core)

    pl.semaphore_wait(barrier, len(partners))

    pending = []
    sib_base = []
    for tick in range(TICKS):
        sib_base.append(send(
            other_base.at[tick], base.at[tick, chip, my_rows],
            sib_send.at[tick], sib_recv.at[tick], sibling,
        ))
        if tick == 0:
            sib_code = send(code_own, code_sib, sib_send.at[3], sib_recv.at[3], sibling)
    sib_tile = send(tile_blocks.at[0, 0], weights.at[tile_rows], sib_send.at[4], sib_recv.at[4], sibling)
    sib_diag = send(diag_inverse.at[0], weights.at[diag_rows], sib_send.at[5], sib_recv.at[5], sibling)
    pending += sib_base + [sib_code, sib_tile, sib_diag]

    def gather_base(tick):
        sib_base[tick].wait_recv()
        copies = []
        for n, (a, b) in enumerate(SPREAD):
            copies.append(send(
                base.at[tick, chip], base.at[tick, chip],
                base_send.at[tick, n], base_recv.at[tick, n], at(s, a, b),
            ))
        pending.extend(copies)
        return copies

    arriving = gather_base(0)

    sib_code.wait_recv()
    code_send[...] = code_own[...] + code_sib[...]
    code_copies = {}
    for d in RING:
        code_copies[d] = send(code_send, codes.at[0, d], code_s1.at[d], code_r1.at[d], at(up, d, 0))
    pending.extend(code_copies.values())
    loads[3].wait()
    loads[4].wait()
    sib_tile.wait_recv()
    sib_diag.wait_recv()
    for b in range(CHIPS):
        blocks[b] = weights[:, b * TILE:(b + 1) * TILE]
    code_moves = []
    for d in RING:
        code_copies[d].wait_recv()
        for e in HOPS:
            code_moves.append(send(codes.at[0, d], codes.at[e, d], code_s2.at[e, d], code_r2.at[e, d], at(s, 0, e)))
    pending.extend(code_moves)
    for copy in arriving:
        copy.wait_recv()

    def dot(a, b):
        return jnp.dot(a, b, preferred_element_type=F32)

    def base_rows(tick):
        return base[tick].reshape(W, LANES)

    def product_rows(tick, e):
        return products[tick, e].reshape(SIDE * 2 * TILE, LANES)

    def placed_part(rows, e):
        return placed[rows, e * 1024:(e + 1) * 1024]

    TOP = slice(0, 2 * TILE)
    LOW = slice(2 * TILE, 3 * TILE)

    def send_products(tick):
        copies = {}
        for d in RING:
            copies[d] = send(
                own_products.at[tick], products.at[tick, 0, d],
                ring_s1.at[tick, d], ring_r1.at[tick, d], at(up, d, 0),
            )
        pending.extend(copies.values())
        return copies

    def forward_products(tick, copies):
        moves = {}
        for d in RING:
            copies[d].wait_recv()
            for e in HOPS:
                moves[e, d] = send(
                    products.at[tick, 0, d], products.at[tick, e, d],
                    ring_s2.at[tick, e, d], ring_r2.at[tick, e, d], at(s, 0, e),
                )
        pending.extend(moves.values())
        return moves

    sib_sol = []

    def give_solution(tick, value):
        lanes = pl.ds(pl.multiple_of(tick * PW + core * LANES, LANES), LANES)
        sol_send[tick] = value
        sol_out[:, lanes] = sol_send[tick, my_rows]
        theirs = pl.ds(pl.multiple_of((1 - core) * HALF, HALF), HALF)
        sib_sol.append(send(
            sol_send.at[tick, theirs], sol_recv.at[tick],
            sib_send.at[6 + tick], sib_recv.at[6 + tick], sibling,
        ))
        pending.append(sib_sol[-1])

    def code_of(e, d, k):
        return jnp.max(codes[e, d, k:k + 1, :])

    back_copies = []

    def give_back(tick):
        total = jnp.zeros((TILE, LANES), F32)
        for e in range(SIDE):
            for d in range(SIDE):
                for k in range(2):
                    part = products[tick, e, d, k * TILE:(k + 1) * TILE].astype(F32)
                    total = total + (code_list[e, d, k] == chip).astype(F32) * part
        back_send[tick] = total
        for h in range(2):
            back_copies.append(send(
                back_send.at[tick, h * HALF:(h + 1) * HALF], back_recv.at[tick, core],
                back_s.at[tick, h], back_r.at[tick, core], (down, chip * 2 + h),
            ))

    own_products[0] = dot(weights[TOP], base_rows(0)).astype(BF16)
    ring = send_products(0)
    arriving = gather_base(1)
    give_solution(0, dot(weights[LOW], base_rows(0)))
    moves = forward_products(0, ring)
    for copy in code_moves:
        copy.wait_recv()
    not_first = (s > 0).astype(F32)
    code_list = {}
    for e in range(SIDE):
        for d in range(SIDE):
            for k in range(2):
                value = code_of(e, d, k)
                code_list[e, d, k] = value
                block = lax.rem(value, CHIPS)
                used = jnp.full((1, LANES), (value < CHIPS).astype(F32) * not_first).astype(BF16)
                at_col = ((e * SIDE + d) * 2 + k) * TILE
                placed[:, at_col:at_col + TILE] = blocks[block] * used

    for tick in range(1, TICKS):
        for copy in arriving:
            copy.wait_recv()
        acc = dot(weights[TOP], base_rows(tick))
        for e in (0,) + HOPS:
            if e:
                for d in RING:
                    moves[e, d].wait_recv()
            acc = acc - dot(placed_part(TOP, e), product_rows(tick - 1, e))
        if tick < TICKS - 1:
            own_products[tick] = acc.astype(BF16)
            ring = send_products(tick)
            arriving = gather_base(tick + 1)
        else:
            code_both = [jnp.max(code_send[k:k + 1, :]) for k in range(2)]
            first_part, second_part = acc[:TILE], acc[TILE:]

            def reduced(target):
                m0 = (code_both[0] == target).astype(F32)
                m1 = (code_both[1] == target).astype(F32)
                return (m0 * first_part + m1 * second_part).astype(BF16)

            reds = []
            for n, (a, b) in enumerate(SPREAD):
                block_send[n] = reduced(chip_at(a, b))
                reds.append(send(block_send.at[n], block_recv.at[n], red_s.at[n], red_r.at[n], at(s, a, b)))
            pending.extend(reds)
            block_recv[CHIPS - 1] = reduced(chip)
        low = dot(weights[LOW], base_rows(tick))
        for e in range(SIDE):
            low = low - dot(placed_part(LOW, e), product_rows(tick - 1, e))
        give_solution(tick, low)
        give_back(tick - 1)
        if tick < TICKS - 1:
            moves = forward_products(tick, ring)

    for copy in reds:
        copy.wait_recv()
    total = jnp.zeros((TILE, LANES), F32)
    for n in range(CHIPS):
        total = total + block_recv[n].astype(F32)
    last_send[...] = total
    mine = pl.ds(pl.multiple_of((TICKS - 1) * PW + core * LANES, LANES), LANES)
    upd_out[:, mine] = last_send[my_rows]
    theirs = pl.ds(pl.multiple_of((1 - core) * HALF, HALF), HALF)
    last = send(last_send.at[theirs], last_recv, sib_send.at[9], sib_recv.at[9], sibling)
    pending.append(last)
    for tick in range(TICKS):
        lanes = pl.ds(pl.multiple_of(tick * PW + (1 - core) * LANES, LANES), LANES)
        sib_sol[tick].wait_recv()
        sol_out[:, lanes] = sol_recv[tick]
    for tick in range(TICKS - 1):
        for k in range(2):
            pltpu.make_async_copy(back_recv.at[tick, k], back_recv.at[tick, k], back_r.at[tick, k]).wait()
            upd_out[:, tick * PW + k * LANES:tick * PW + (k + 1) * LANES] = back_recv[tick, k]
    last.wait_recv()
    other = pl.ds(pl.multiple_of((TICKS - 1) * PW + (1 - core) * LANES, LANES), LANES)
    upd_out[:, other] = last_recv[...]
    for copy in pending + back_copies:
        copy.wait_send()


def body(*arrays):
    right_side = arrays[0]
    rows, width = right_side.shape
    dma = pltpu.SemaphoreType.DMA
    any_spec = pl.BlockSpec(memory_space=pl.ANY)
    smem = pl.BlockSpec(memory_space=pltpu.SMEM)
    vmem = pl.BlockSpec(memory_space=pltpu.VMEM)
    out = jax.ShapeDtypeStruct((rows, width), F32)
    n = len(SPREAD)
    return pl.pallas_call(
        kernel,
        out_shape=(out, out),
        in_specs=[any_spec] * 5 + [smem] * 3,
        out_specs=(vmem, vmem),
        scratch_shapes=[
            pltpu.VMEM((rows, width), BF16),
            pltpu.VMEM((rows, PW), F32),
            pltpu.VMEM((rows, 2 * PW), F32),
            pltpu.VMEM((3 * TILE, W), BF16),
            pltpu.VMEM((CHIPS, 3 * TILE, LANES), BF16),
            pltpu.VMEM((3 * TILE, 2 * W), BF16),
            pltpu.VMEM((TICKS, CHIPS, TILE, LANES), BF16),
            pltpu.VMEM((TICKS, HALF, LANES), BF16),
            pltpu.VMEM((TICKS - 1, SIDE, SIDE, 2 * TILE, LANES), BF16),
            pltpu.VMEM((TICKS - 1, 2 * TILE, LANES), BF16),
            pltpu.VMEM((8, LANES), jnp.int32),
            pltpu.VMEM((8, LANES), jnp.int32),
            pltpu.VMEM((8, LANES), jnp.int32),
            pltpu.VMEM((SIDE, SIDE, 8, LANES), jnp.int32),
            pltpu.VMEM((TICKS, TILE, LANES), F32),
            pltpu.VMEM((TICKS, HALF, LANES), F32),
            pltpu.VMEM((TICKS - 1, TILE, LANES), F32),
            pltpu.VMEM((TICKS - 1, 2, HALF, LANES), F32),
            pltpu.VMEM((n, TILE, LANES), BF16),
            pltpu.VMEM((CHIPS, TILE, LANES), BF16),
            pltpu.VMEM((TILE, LANES), F32),
            pltpu.VMEM((HALF, LANES), F32),
            dma((5,)), dma((10,)), dma((10,)),
            dma((TICKS, n)), dma((TICKS, n)),
            dma((SIDE,)), dma((SIDE,)), dma((SIDE, SIDE)), dma((SIDE, SIDE)),
            dma((2, SIDE)), dma((2, SIDE)), dma((2, SIDE, SIDE)), dma((2, SIDE, SIDE)),
            dma((2, 2)), dma((2, 2)),
            dma((n,)), dma((n,)),
        ],
        compiler_params=pltpu.CompilerParams(collective_id=0, has_side_effects=True),
        name="chain_solve",
    )(*arrays)


def solution(mesh):
    placed = (
        P(("chain", "rows"), None),
        P(("chain", "rows"), None),
        P("rows", None),
        P("chain", "rows", None),
        P("chain", "rows", None, None),
        P("chain", "rows"),
        P("chain", None),
        P("chain"),
    )
    return jax.shard_map(
        body,
        mesh=mesh,
        in_specs=placed,
        out_specs=(P(("chain", "rows"), None), P(("chain", "rows"), None)),
        check_vma=False,
    )
```

```python
import jax
import jax.numpy as jnp
from jax import lax
from jax.experimental import pallas as pl
from jax.experimental.pallas import tpu as pltpu
from jax.sharding import PartitionSpec as P

PW = 256
TILE = 128
HALF = 64
W = 2048
NZ = 8
SIDE = 4
CHIPS = SIDE * SIDE
TICKS = 3
LANES = 128
F32 = jnp.float32
BF16 = jnp.bfloat16
MESH = pl.DeviceIdType.MESH
HOPS = (1, 3, 2)
RING = (0,) + HOPS
FAR_FIRST = tuple((a, b) for a in range(SIDE - 1, -1, -1) for b in range(SIDE - 1, -1, -1) if (a, b) != (0, 0))
NODES = tuple((f, e) for e in RING for f in range(SIDE))
ROOTS = ((0, 0), (1, 0), (3, 0), (2, 0))
EVENTS = tuple(((f, 0), tuple((f, e) for e in HOPS)) for f in RING)
CHUNK = 8


def slot(f, e):
    return NODES.index((f, e))


def kernel(
    right_side, entering, first_updates, diag_inverse, tile_blocks, targets_in, order_in, count_in,
    sol_out, upd_out,
    targets, order, count, code_table,
    given, enter, first, weights, blocks, placed, base, other_base, products, own_products, acc,
    code_own, code_sib, code_send, codes, sol_send, sol_recv, back_send, back_recv,
    block_send, block_recv,
    load_sem, sib_send, sib_recv, base_s, base_r, code_s, code_r,
    ring_s, ring_r, back_s, back_r, red_s, red_r,
):
    s = lax.axis_index("chain")
    row = lax.axis_index("rows")
    core = lax.rem(row, 2)
    chip = row // 2
    x = lax.rem(chip, SIDE)
    y = chip // SIDE
    p1 = x + core * (y - x)
    p2 = y + core * (x - y)
    stride1 = 1 + 3 * core
    stride2 = 4 - 3 * core
    up = lax.rem(s + 1, NZ)
    down = lax.rem(s + NZ - 1, NZ)
    sibling = (s, row + 1 - 2 * core)

    def chip_at(d1, d2):
        return lax.rem(p1 + d1 + SIDE, SIDE) * stride1 + lax.rem(p2 + d2 + SIDE, SIDE) * stride2

    def at(plane, d1, d2):
        return (plane, chip_at(d1, d2) * 2 + core)

    def across(plane, d1, d2):
        return (plane, chip_at(d1, d2) * 2 + 1 - core)

    def remote(src, dst, ssem, rsem, device):
        return pltpu.make_async_remote_copy(
            src_ref=src, dst_ref=dst, send_sem=ssem, recv_sem=rsem,
            device_id=device, device_id_type=MESH,
        )

    def drain(ref, sem):
        pltpu.make_async_copy(ref, ref, sem).wait()

    barrier = pltpu.get_barrier_semaphore()

    def greet(device):
        pl.semaphore_signal(barrier, inc=1, device_id=device, device_id_type=MESH)

    greet(sibling)
    for a, b in FAR_FIRST:
        greet(at(s, a, b))
        greet(across(s, a, b))
    in_plane = 1 + 2 * len(FAR_FIRST)
    z_moves = [(f, 0) for f, _ in ROOTS] + [(0, f) for f, _ in ROOTS if f]
    in_z = len(z_moves) + 1
    for a, b in z_moves:
        greet(at(up, a, b))
        greet(at(down, SIDE - a, SIDE - b))
    greet(across(up, 0, 0))
    greet(across(down, 0, 0))

    my_rows = pl.ds(pl.multiple_of(core * HALF, HALF), HALF)
    their_rows = pl.ds(pl.multiple_of((1 - core) * HALF, HALF), HALF)
    tile_rows = pl.ds(pl.multiple_of(core * TILE, TILE), TILE)
    diag_rows = pl.ds(pl.multiple_of(2 * TILE + core * HALF, HALF), HALF)
    loads = [
        pltpu.make_async_copy(right_side, given, load_sem.at[0]),
        pltpu.make_async_copy(entering, enter, load_sem.at[1]),
        pltpu.make_async_copy(first_updates, first, load_sem.at[2]),
        pltpu.make_async_copy(targets_in, targets, load_sem.at[3]),
        pltpu.make_async_copy(order_in, order, load_sem.at[4]),
        pltpu.make_async_copy(count_in, count, load_sem.at[5]),
        pltpu.make_async_copy(tile_blocks.at[0, 0], weights.at[tile_rows], load_sem.at[6]),
        pltpu.make_async_copy(diag_inverse.at[0], weights.at[diag_rows], load_sem.at[7]),
    ]
    for copy in loads:
        copy.start()
    for copy in loads[:3]:
        copy.wait()
    is_first = (s == 0).astype(F32)

    def head_part(tick, half):
        lanes = pl.ds(pl.multiple_of(tick * PW + half * LANES, LANES), LANES)
        value = given[:, lanes].astype(F32)
        if tick == 0:
            taken = enter[:, pl.ds(pl.multiple_of(half * LANES, LANES), LANES)]
        else:
            lanes = pl.ds(pl.multiple_of((tick - 1) * PW + half * LANES, LANES), LANES)
            taken = is_first * first[:, lanes]
        return (value - taken).astype(BF16)

    for tick in range(TICKS):
        other_base[tick] = head_part(tick, 1 - core)
        base[tick, chip, my_rows] = head_part(tick, core)

    for copy in loads[3:6]:
        copy.wait()
    live = jnp.int32(0)
    for k in range(order.shape[1]):
        hit = jnp.logical_and(order[0, k] == row, k < count[0])
        live = live + hit.astype(jnp.int32)
    code = targets[0, 0] + CHIPS * (1 - live)
    code_rows = lax.broadcasted_iota(jnp.int32, (8, LANES), 0)
    code_own[...] = jnp.where(code_rows == core, code, 0)

    pl.semaphore_wait(barrier, in_plane + 2 * in_z)

    def sib_base(tick):
        return remote(
            other_base.at[tick], base.at[tick, chip, my_rows],
            sib_send.at[0], sib_recv.at[tick], sibling,
        )

    def sib_code():
        return remote(code_own, code_sib, sib_send.at[1], sib_recv.at[3], sibling)

    def sib_tile():
        return remote(tile_blocks.at[0, 0], weights.at[tile_rows], sib_send.at[2], sib_recv.at[4], sibling)

    def sib_diag():
        return remote(diag_inverse.at[0], weights.at[diag_rows], sib_send.at[3], sib_recv.at[5], sibling)

    def base_half(rows, d1, d2):
        return remote(
            base.at[0, chip, rows], base.at[0, chip, rows],
            base_s, base_r.at[0, 0], at(s, d1, d2),
        )

    n_far = len(FAR_FIRST)
    sib_base(0).start()
    sib_code().start()
    for a, b in FAR_FIRST:
        base_half(my_rows, a, b).start()
    sib_base(0).wait_recv()
    for a, b in FAR_FIRST:
        base_half(their_rows, b, a).start()
    sib_base(1).start()
    sib_base(2).start()

    def code_root(f, e):
        return remote(code_send, codes.at[slot(f, e)], code_s, code_r.at[0], at(up, f, e))

    def code_edge(node, child):
        n, m = slot(*node), slot(*child)
        return remote(
            codes.at[n], codes.at[m], code_s, code_r.at[1],
            at(s, child[0] - node[0], child[1] - node[1]),
        )

    sib_code().wait_recv()
    code_send[...] = code_own[...] + code_sib[...]

    for f, e in ROOTS:
        code_root(f, e).start()

    sib_tile().start()
    sib_diag().start()

    def base_copy(tick, node, child):
        held = chip_at(-node[0], -node[1])
        return remote(
            base.at[tick, held], base.at[tick, held], base_s, base_r.at[tick, int(child[1] > 0)],
            at(s, child[0] - node[0], child[1] - node[1]),
        )

    def base_along(tick):
        sib_base(tick).wait_recv()
        for f in HOPS:
            base_copy(tick, (0, 0), (f, 0)).start()

    def base_over(tick):
        drain(base.at[tick, :SIDE - 1], base_r.at[tick, 0])
        for f in RING:
            for e in HOPS:
                base_copy(tick, (f, 0), (f, e)).start()

    def base_done(tick):
        drain(base.at[tick, :CHIPS - SIDE], base_r.at[tick, 1])

    base_along(1)
    for copy in loads[6:]:
        copy.wait()
    sib_tile().wait_recv()
    sib_diag().wait_recv()
    for b in range(CHIPS):
        blocks[b] = weights[:, b * TILE:(b + 1) * TILE]

    drain(codes.at[:SIDE], code_r.at[0])
    for node, children in EVENTS:
        for child in children:
            code_edge(node, child).start()

    drain(base.at[0, :n_far], base_r.at[0, 0])

    def dot(a, b):
        return jnp.dot(a, b, preferred_element_type=F32)

    def base_rows(tick):
        return base[tick].reshape(W, LANES)

    TOP = slice(0, 2 * TILE)
    LOW = slice(2 * TILE, 3 * TILE)
    def placed_dot(rows, tick, k, part):
        first_slot = part * CHUNK
        col = (k * CHIPS + first_slot) * TILE
        right = products[tick, k, first_slot:first_slot + CHUNK].reshape(CHUNK * TILE, LANES)
        return dot(placed[rows, col:col + CHUNK * TILE], right)

    def move(k, f, e):
        return (f, e) if k == 0 else (e, f)

    def root(tick, k, node):
        n = slot(*node)
        return remote(
            own_products.at[tick, k], products.at[tick, k, n],
            ring_s, ring_r.at[tick, k, n], at(up, *move(k, *node)),
        )

    def edge(tick, k, node, child):
        n, m = slot(*node), slot(*child)
        return remote(
            products.at[tick, k, n], products.at[tick, k, m],
            ring_s, ring_r.at[tick, k, m if m < SIDE else SIDE + m // CHUNK],
            at(s, *move(k, child[0] - node[0], child[1] - node[1])),
        )

    def parts_in(tick, k, part):
        drain(products.at[tick, k, max(part * CHUNK, SIDE):(part + 1) * CHUNK], ring_r.at[tick, k, SIDE + part])

    def pass_on(tick):
        for j, (node, children) in enumerate(EVENTS):
            for k in range(2):
                drain(products.at[tick, k, slot(*node)], ring_r.at[tick, k, slot(*node)])
                for child in children:
                    edge(tick, k, node, child).start()

    def take_products(tick):
        for part in range(2):
            for k in range(2):
                parts_in(tick, k, part)
                acc[...] = acc[...] - placed_dot(TOP, tick, k, part)

    def give_back(tick):
        total = jnp.zeros((TILE, LANES), F32)
        for k in range(2):
            for n in range(CHIPS):
                part = products[tick, k, n].astype(F32)
                total = total + (code_table[k * CHIPS + n] == chip).astype(F32) * part
        back_send[tick] = total
        for h in range(2):
            back(tick, h, core).start()

    def back(tick, h, k):
        return remote(
            back_send.at[tick, h * HALF:(h + 1) * HALF], back_recv.at[tick, k],
            back_s, back_r, (down, chip * 2 + h),
        )

    code_both = [jnp.max(code_send[k:k + 1, :]) for k in range(2)]

    def own_half(n, a, b):
        return remote(
            block_send.at[n, my_rows], block_recv.at[core * CHIPS + n],
            red_s, red_r, at(s, a, b),
        )

    def other_half(n, a, b):
        return remote(
            block_send.at[n, their_rows], block_recv.at[core * CHIPS + n],
            red_s, red_r, across(s, a, b),
        )

    def reduce_out(tick):
        def reduced(target):
            m0 = (code_both[0] == target).astype(F32)
            m1 = (code_both[1] == target).astype(F32)
            return (m0 * acc[:TILE] + m1 * acc[TILE:]).astype(BF16)

        for n, (a, b) in enumerate(FAR_FIRST):
            block_send[n] = reduced(chip_at(a, b))
            own_half(n, a, b).start()
        block_send[n_far] = reduced(chip)
        other_half(n_far, 0, 0).start()
        for b, a in FAR_FIRST:
            n = FAR_FIRST.index((a, b))
            other_half(n, a, b).start()
        block_recv[core * CHIPS + n_far] = block_send[n_far, my_rows]

    def reduce_in(tick):
        drain(block_recv.at[:2 * CHIPS - 1], red_r)
        for k in range(2):
            total = jnp.zeros((HALF, LANES), F32)
            for n in range(CHIPS):
                total = total + block_recv[k * CHIPS + n].astype(F32)
            upd_out[:, tick * PW + k * LANES:tick * PW + (k + 1) * LANES] = total

    def sib_sol(tick):
        return remote(
            sol_send.at[tick, their_rows], sol_recv.at[tick],
            sib_send.at[4], sib_recv.at[6], sibling,
        )

    inner = s > 0

    def read_codes():
        drain(codes.at[SIDE:], code_r.at[1])
        for k in range(2):
            for n, (f, e) in enumerate(NODES):
                value = jnp.max(codes[slot(*move(k, f, e)), k:k + 1, :])
                code_table[k * CHIPS + n] = value
                block = lax.rem(value, CHIPS)
                used = jnp.full((1, LANES), (value < CHIPS).astype(F32)).astype(BF16)
                col = (k * CHIPS + n) * TILE
                placed[:, col:col + TILE] = blocks[block] * used

    for tick in range(TICKS):
        if tick:
            base_done(tick)
        acc[...] = dot(weights[TOP], base_rows(tick))
        if tick:
            @pl.when(inner)
            def _():
                take_products(tick - 1)
        if tick < TICKS - 1:
            for k in range(2):
                own_products[tick, k] = acc[k * TILE:(k + 1) * TILE].astype(BF16)
            for node in ROOTS:
                for k in range(2):
                    root(tick, k, node).start()
            base_over(tick + 1)
            if tick + 2 < TICKS:
                base_along(tick + 2)
        else:
            reduce_out(tick)
        sol_send[tick] = dot(weights[LOW], base_rows(tick))
        if tick:
            @pl.when(inner)
            def _():
                for k in range(2):
                    for part in range(2):
                        sol_send[tick] = sol_send[tick] - placed_dot(LOW, tick - 1, k, part)
                give_back(tick - 1)
        lanes = pl.ds(pl.multiple_of(tick * PW + core * LANES, LANES), LANES)
        sol_out[:, lanes] = sol_send[tick, my_rows]
        sib_sol(tick).start()
        if tick < TICKS - 1:
            @pl.when(inner)
            def _():
                pass_on(tick)
        if tick == 0:
            read_codes()
        if tick == 1:
            @pl.when(s == 0)
            def _():
                pass_on(0)

    @pl.when(s == 0)
    def _():
        for tick in range(TICKS - 1):
            if tick:
                pass_on(tick)
            for k in range(2):
                for part in range(2):
                    parts_in(tick, k, part)
            give_back(tick)

    drain(back_recv, back_r)
    for tick in range(TICKS - 1):
        for k in range(2):
            upd_out[:, tick * PW + k * LANES:tick * PW + (k + 1) * LANES] = back_recv[tick, k]
    drain(sol_recv, sib_recv.at[6])
    for tick in range(TICKS):
        lanes = pl.ds(pl.multiple_of(tick * PW + (1 - core) * LANES, LANES), LANES)
        sol_out[:, lanes] = sol_recv[tick]
    reduce_in(TICKS - 1)
    drain(other_base, sib_send.at[0])
    drain(code_own, sib_send.at[1])
    drain(weights.at[:TILE], sib_send.at[2])
    drain(weights.at[:HALF], sib_send.at[3])
    drain(sol_recv, sib_send.at[4])
    drain(base.at[:, :n_far], base_s)
    drain(codes, code_s)
    drain(products, ring_s)
    drain(back_send, back_s)
    drain(block_recv.at[:2 * CHIPS - 1], red_s)


def body(*arrays):
    right_side = arrays[0]
    rows, width = right_side.shape
    dma = pltpu.SemaphoreType.DMA
    any_spec = pl.BlockSpec(memory_space=pl.ANY)
    hbm_spec = pl.BlockSpec(memory_space=pltpu.HBM)
    vmem = pl.BlockSpec(memory_space=pltpu.VMEM)
    out = jax.ShapeDtypeStruct((rows, width), F32)
    return pl.pallas_call(
        kernel,
        out_shape=(out, out),
        in_specs=[any_spec] * 5 + [hbm_spec] * 3,
        out_specs=(vmem, vmem),
        scratch_shapes=[
            pltpu.SMEM(arrays[5].shape, jnp.int32),
            pltpu.SMEM(arrays[6].shape, jnp.int32),
            pltpu.SMEM(arrays[7].shape, jnp.int32),
            pltpu.SMEM((2 * CHIPS,), jnp.int32),
            pltpu.VMEM((rows, width), BF16),
            pltpu.VMEM((rows, PW), F32),
            pltpu.VMEM((rows, 2 * PW), F32),
            pltpu.VMEM((3 * TILE, W), BF16),
            pltpu.VMEM((CHIPS, 3 * TILE, LANES), BF16),
            pltpu.VMEM((3 * TILE, 2 * W), BF16),
            pltpu.VMEM((TICKS, CHIPS, TILE, LANES), BF16),
            pltpu.VMEM((TICKS, HALF, LANES), BF16),
            pltpu.VMEM((TICKS - 1, 2, CHIPS, TILE, LANES), BF16),
            pltpu.VMEM((TICKS - 1, 2, TILE, LANES), BF16),
            pltpu.VMEM((2 * TILE, LANES), F32),
            pltpu.VMEM((8, LANES), jnp.int32),
            pltpu.VMEM((8, LANES), jnp.int32),
            pltpu.VMEM((8, LANES), jnp.int32),
            pltpu.VMEM((CHIPS, 8, LANES), jnp.int32),
            pltpu.VMEM((TICKS, TILE, LANES), F32),
            pltpu.VMEM((TICKS, HALF, LANES), F32),
            pltpu.VMEM((TICKS - 1, TILE, LANES), F32),
            pltpu.VMEM((TICKS - 1, 2, HALF, LANES), F32),
            pltpu.VMEM((CHIPS, TILE, LANES), BF16),
            pltpu.VMEM((2 * CHIPS, HALF, LANES), BF16),
            dma((8,)), dma((5,)), dma((7,)),
            dma, dma((TICKS, 2)), dma, dma((2,)),
            dma, dma((2, 2, SIDE + 2)), dma, dma, dma, dma,
        ],
        compiler_params=pltpu.CompilerParams(collective_id=0, has_side_effects=True),
        name="chain_solve",
    )(*arrays)


def solution(mesh):
    placed = (
        P(("chain", "rows"), None),
        P(("chain", "rows"), None),
        P("rows", None),
        P("chain", "rows", None),
        P("chain", "rows", None, None),
        P("chain", "rows"),
        P("chain", None),
        P("chain"),
    )
    return jax.shard_map(
        body,
        mesh=mesh,
        in_specs=placed,
        out_specs=(P(("chain", "rows"), None), P(("chain", "rows"), None)),
        check_vma=False,
    )
```

```python
import jax
import jax.numpy as jnp
from jax import lax
from jax.experimental import pallas as pl
from jax.experimental.pallas import tpu as pltpu
from jax.sharding import PartitionSpec as P

PW = 256
TILE = 128
HALF = 64
W = 2048
NZ = 8
SIDE = 4
CHIPS = SIDE * SIDE
TICKS = 3
LANES = 128
F32 = jnp.float32
BF16 = jnp.bfloat16
MESH = pl.DeviceIdType.MESH
HOPS = (1, 3, 2)
RING = (0,) + HOPS
FAR_FIRST = tuple((a, b) for a in range(SIDE - 1, -1, -1) for b in range(SIDE - 1, -1, -1) if (a, b) != (0, 0))
NODES = tuple((f, e) for e in RING for f in range(SIDE))
ROOTS = ((0, 0), (1, 0), (3, 0), (2, 0))
EVENTS = tuple(((f, 0), tuple((f, e) for e in HOPS)) for f in RING)
CHUNK = 8


def slot(f, e):
    return NODES.index((f, e))


def kernel(
    right_side, entering, first_updates, diag_inverse, tile_blocks, targets_in, order_in, count_in,
    sol_out, upd_out,
    targets, order, count, code_table,
    given, enter, first, weights, blocks, placed, base, other_base, products, own_products, acc,
    code_own, code_sib, code_send, codes, sol_send, sol_recv, back_send, back_recv,
    block_send, block_recv,
    load_sem, sib_send, sib_recv, base_s, base_r, code_s, code_r,
    ring_s, ring_r, back_s, back_r, red_s, red_r, last_in,
):
    s = lax.axis_index("chain")
    row = lax.axis_index("rows")
    core = lax.rem(row, 2)
    chip = row // 2
    x = lax.rem(chip, SIDE)
    y = chip // SIDE
    p1 = x + core * (y - x)
    p2 = y + core * (x - y)
    stride1 = 1 + 3 * core
    stride2 = 4 - 3 * core
    up = lax.rem(s + 1, NZ)
    down = lax.rem(s + NZ - 1, NZ)
    sibling = (s, row + 1 - 2 * core)

    def chip_at(d1, d2):
        return lax.rem(p1 + d1 + SIDE, SIDE) * stride1 + lax.rem(p2 + d2 + SIDE, SIDE) * stride2

    def at(plane, d1, d2):
        return (plane, chip_at(d1, d2) * 2 + core)

    def across(plane, d1, d2):
        return (plane, chip_at(d1, d2) * 2 + 1 - core)

    def remote(src, dst, ssem, rsem, device):
        return pltpu.make_async_remote_copy(
            src_ref=src, dst_ref=dst, send_sem=ssem, recv_sem=rsem,
            device_id=device, device_id_type=MESH,
        )

    def drain(ref, sem):
        pltpu.make_async_copy(ref, ref, sem).wait()

    barrier = pltpu.get_barrier_semaphore()

    def greet(device):
        pl.semaphore_signal(barrier, inc=1, device_id=device, device_id_type=MESH)

    greet(sibling)
    for a, b in FAR_FIRST:
        greet(at(s, a, b))
        greet(across(s, a, b))
    in_plane = 1 + 2 * len(FAR_FIRST)
    z_moves = [(f, 0) for f, _ in ROOTS] + [(0, f) for f, _ in ROOTS if f]
    in_z = len(z_moves) + 1
    for a, b in z_moves:
        greet(at(down, SIDE - a, SIDE - b))
    greet(across(down, 0, 0))

    @pl.when(s < NZ - 1)
    def _():
        for a, b in z_moves:
            greet(at(up, a, b))
        greet(across(up, 0, 0))

    my_rows = pl.ds(pl.multiple_of(core * HALF, HALF), HALF)
    their_rows = pl.ds(pl.multiple_of((1 - core) * HALF, HALF), HALF)
    tile_rows = pl.ds(pl.multiple_of(core * TILE, TILE), TILE)
    diag_rows = pl.ds(pl.multiple_of(2 * TILE + core * HALF, HALF), HALF)
    loads = [
        pltpu.make_async_copy(right_side, given, load_sem.at[0]),
        pltpu.make_async_copy(entering, enter, load_sem.at[1]),
        pltpu.make_async_copy(first_updates, first, load_sem.at[2]),
        pltpu.make_async_copy(targets_in, targets, load_sem.at[3]),
        pltpu.make_async_copy(order_in, order, load_sem.at[4]),
        pltpu.make_async_copy(count_in, count, load_sem.at[5]),
        pltpu.make_async_copy(tile_blocks.at[0, 0], weights.at[tile_rows], load_sem.at[6]),
        pltpu.make_async_copy(diag_inverse.at[0], weights.at[diag_rows], load_sem.at[7]),
    ]
    for copy in loads:
        copy.start()
    for copy in loads[:3]:
        copy.wait()
    is_first = (s == 0).astype(F32)

    def head_part(tick, half):
        lanes = pl.ds(pl.multiple_of(tick * PW + half * LANES, LANES), LANES)
        value = given[:, lanes].astype(F32)
        if tick == 0:
            taken = enter[:, pl.ds(pl.multiple_of(half * LANES, LANES), LANES)]
        else:
            lanes = pl.ds(pl.multiple_of((tick - 1) * PW + half * LANES, LANES), LANES)
            taken = is_first * first[:, lanes]
        return (value - taken).astype(BF16)

    for tick in range(TICKS):
        other_base[tick] = head_part(tick, 1 - core)
        base[tick, chip, my_rows] = head_part(tick, core)

    for copy in loads[3:6]:
        copy.wait()
    live = jnp.int32(0)
    for k in range(order.shape[1]):
        hit = jnp.logical_and(order[0, k] == row, k < count[0])
        live = live + hit.astype(jnp.int32)
    code = targets[0, 0] + CHIPS * (1 - live)
    code_rows = lax.broadcasted_iota(jnp.int32, (8, LANES), 0)
    code_own[...] = jnp.where(code_rows == core, code, 0)

    pl.semaphore_wait(barrier, in_plane + in_z + in_z * (s > 0).astype(jnp.int32))

    @pl.when(s == NZ - 1)
    def _():
        for device in (at(up, 0, 0), across(up, 0, 0)):
            pl.semaphore_signal(last_in, inc=1, device_id=device, device_id_type=MESH)

    def sib_base(tick):
        return remote(
            other_base.at[tick], base.at[tick, chip, my_rows],
            sib_send.at[0], sib_recv.at[tick], sibling,
        )

    def sib_code():
        return remote(code_own, code_sib, sib_send.at[1], sib_recv.at[3], sibling)

    def sib_tile():
        return remote(tile_blocks.at[0, 0], weights.at[tile_rows], sib_send.at[2], sib_recv.at[4], sibling)

    def sib_diag():
        return remote(diag_inverse.at[0], weights.at[diag_rows], sib_send.at[3], sib_recv.at[5], sibling)

    def base_half(rows, d1, d2):
        return remote(
            base.at[0, chip, rows], base.at[0, chip, rows],
            base_s, base_r.at[0, 0], at(s, d1, d2),
        )

    n_far = len(FAR_FIRST)
    sib_base(0).start()
    sib_code().start()
    for a, b in FAR_FIRST:
        base_half(my_rows, a, b).start()
    sib_base(0).wait_recv()
    for a, b in FAR_FIRST:
        base_half(their_rows, b, a).start()
    sib_base(1).start()
    sib_base(2).start()

    def code_root(f, e):
        return remote(code_send, codes.at[slot(f, e)], code_s, code_r.at[0], at(up, f, e))

    def code_edge(node, child):
        n, m = slot(*node), slot(*child)
        return remote(
            codes.at[n], codes.at[m], code_s, code_r.at[1],
            at(s, child[0] - node[0], child[1] - node[1]),
        )

    sib_code().wait_recv()
    code_send[...] = code_own[...] + code_sib[...]

    for f, e in ROOTS:
        code_root(f, e).start()

    sib_tile().start()
    sib_diag().start()

    def base_copy(tick, node, child):
        held = chip_at(-node[0], -node[1])
        return remote(
            base.at[tick, held], base.at[tick, held], base_s, base_r.at[tick, int(child[1] > 0)],
            at(s, child[0] - node[0], child[1] - node[1]),
        )

    def base_along(tick):
        sib_base(tick).wait_recv()
        for f in HOPS:
            base_copy(tick, (0, 0), (f, 0)).start()

    def base_over(tick, rings=RING):
        if rings[0] == 0:
            drain(base.at[tick, :SIDE - 1], base_r.at[tick, 0])
        for f in rings:
            for e in HOPS:
                base_copy(tick, (f, 0), (f, e)).start()

    def base_done(tick):
        drain(base.at[tick, :CHIPS - SIDE], base_r.at[tick, 1])

    base_along(1)
    base_along(2)
    for copy in loads[6:]:
        copy.wait()
    sib_tile().wait_recv()
    sib_diag().wait_recv()
    for b in range(CHIPS):
        blocks[b] = weights[:, b * TILE:(b + 1) * TILE]

    def pass_codes():
        drain(codes.at[:SIDE], code_r.at[0])
        for node, children in EVENTS:
            for child in children:
                code_edge(node, child).start()

    @pl.when(s > 0)
    def _():
        pass_codes()


    base_over(1, RING)
    drain(base.at[0, :n_far], base_r.at[0, 0])

    def dot(a, b):
        return jnp.dot(a, b, preferred_element_type=F32)

    def base_rows(tick):
        return base[tick].reshape(W, LANES)

    TOP = slice(0, 2 * TILE)
    LOW = slice(2 * TILE, 3 * TILE)
    def placed_dot(rows, tick, k, part):
        first_slot = part * CHUNK
        col = (k * CHIPS + first_slot) * TILE
        right = products[tick, k, first_slot:first_slot + CHUNK].reshape(CHUNK * TILE, LANES)
        return dot(placed[rows, col:col + CHUNK * TILE], right)

    def move(k, f, e):
        return (f, e) if k == 0 else (e, f)

    def root(tick, k, node):
        n = slot(*node)
        return remote(
            own_products.at[tick, k], products.at[tick, k, n],
            ring_s, ring_r.at[tick, k, n], at(up, *move(k, *node)),
        )

    def edge(tick, k, node, child):
        n, m = slot(*node), slot(*child)
        return remote(
            products.at[tick, k, n], products.at[tick, k, m],
            ring_s, ring_r.at[tick, k, m if m < SIDE else SIDE + m // CHUNK],
            at(s, *move(k, child[0] - node[0], child[1] - node[1])),
        )

    def parts_in(tick, k, part):
        drain(products.at[tick, k, max(part * CHUNK, SIDE):(part + 1) * CHUNK], ring_r.at[tick, k, SIDE + part])

    def pass_on(tick):
        for j, (node, children) in enumerate(EVENTS):
            for k in range(2):
                drain(products.at[tick, k, slot(*node)], ring_r.at[tick, k, slot(*node)])
                for child in children:
                    edge(tick, k, node, child).start()

    def take_products(tick):
        for part in range(2):
            for k in range(2):
                parts_in(tick, k, part)
                acc[...] = acc[...] - placed_dot(TOP, tick, k, part)

    def give_back(tick):
        total = jnp.zeros((TILE, LANES), F32)
        for k in range(2):
            for n in range(CHIPS):
                part = products[tick, k, n].astype(F32)
                total = total + (code_table[k * CHIPS + n] == chip).astype(F32) * part
        back_send[tick] = total
        for h in range(2):
            back(tick, h, core).start()

    def back(tick, h, k):
        return remote(
            back_send.at[tick, h * HALF:(h + 1) * HALF], back_recv.at[tick, k],
            back_s, back_r, (down, chip * 2 + h),
        )

    code_both = [jnp.max(code_send[k:k + 1, :]) for k in range(2)]

    def own_half(n, a, b):
        return remote(
            block_send.at[n, my_rows], block_recv.at[core * CHIPS + n],
            red_s, red_r, at(s, a, b),
        )

    def other_half(n, a, b):
        return remote(
            block_send.at[n, their_rows], block_recv.at[core * CHIPS + n],
            red_s, red_r, across(s, a, b),
        )

    def reduce_out(tick):
        def reduced(target):
            m0 = (code_both[0] == target).astype(F32)
            m1 = (code_both[1] == target).astype(F32)
            return (m0 * acc[:TILE] + m1 * acc[TILE:]).astype(BF16)

        for n, (a, b) in enumerate(FAR_FIRST):
            block_send[n] = reduced(chip_at(a, b))
            own_half(n, a, b).start()
        block_send[n_far] = reduced(chip)
        other_half(n_far, 0, 0).start()
        for b, a in FAR_FIRST:
            n = FAR_FIRST.index((a, b))
            other_half(n, a, b).start()
        block_recv[core * CHIPS + n_far] = block_send[n_far, my_rows]

    def reduce_in(tick):
        drain(block_recv.at[:2 * CHIPS - 1], red_r)
        for k in range(2):
            total = jnp.zeros((HALF, LANES), F32)
            for n in range(CHIPS):
                total = total + block_recv[k * CHIPS + n].astype(F32)
            upd_out[:, tick * PW + k * LANES:tick * PW + (k + 1) * LANES] = total

    def sib_sol(tick):
        return remote(
            sol_send.at[tick, their_rows], sol_recv.at[tick],
            sib_send.at[4], sib_recv.at[6], sibling,
        )

    inner = s > 0

    def read_codes(place):
        drain(codes.at[SIDE:], code_r.at[1])
        for k in range(2):
            for n, (f, e) in enumerate(NODES):
                value = jnp.max(codes[slot(*move(k, f, e)), k:k + 1, :])
                code_table[k * CHIPS + n] = value
                if place:
                    block = lax.rem(value, CHIPS)
                    used = jnp.full((1, LANES), (value < CHIPS).astype(F32)).astype(BF16)
                    col = (k * CHIPS + n) * TILE
                    placed[:, col:col + TILE] = blocks[block] * used

    for tick in range(TICKS):
        if tick:
            base_done(tick)
        acc[...] = dot(weights[TOP], base_rows(tick))
        if tick:
            @pl.when(inner)
            def _():
                take_products(tick - 1)
        if tick < TICKS - 1:
            for k in range(2):
                own_products[tick, k] = acc[k * TILE:(k + 1) * TILE].astype(BF16)
            for node in ROOTS:
                for k in range(2):
                    root(tick, k, node).start()
        else:
            reduce_out(tick)
        sol_send[tick] = dot(weights[LOW], base_rows(tick))
        if tick:
            @pl.when(inner)
            def _():
                for k in range(2):
                    for part in range(2):
                        sol_send[tick] = sol_send[tick] - placed_dot(LOW, tick - 1, k, part)
                give_back(tick - 1)
        lanes = pl.ds(pl.multiple_of(tick * PW + core * LANES, LANES), LANES)
        sol_out[:, lanes] = sol_send[tick, my_rows]
        sib_sol(tick).start()
        if tick < TICKS - 1:
            @pl.when(inner)
            def _():
                pass_on(tick)
        if tick == 0:
            base_over(2, RING)
        if tick == 0:
            @pl.when(inner)
            def _():
                read_codes(True)
        if tick == 1:
            @pl.when(s == 0)
            def _():
                pass_codes()
                pass_on(0)

    @pl.when(s == 0)
    def _():
        read_codes(False)
        pl.semaphore_wait(last_in, 2)
        for tick in range(TICKS - 1):
            if tick:
                pass_on(tick)
            for k in range(2):
                for part in range(2):
                    parts_in(tick, k, part)
            give_back(tick)

    drain(back_recv, back_r)
    for tick in range(TICKS - 1):
        for k in range(2):
            upd_out[:, tick * PW + k * LANES:tick * PW + (k + 1) * LANES] = back_recv[tick, k]
    drain(sol_recv, sib_recv.at[6])
    for tick in range(TICKS):
        lanes = pl.ds(pl.multiple_of(tick * PW + (1 - core) * LANES, LANES), LANES)
        sol_out[:, lanes] = sol_recv[tick]
    reduce_in(TICKS - 1)
    drain(other_base, sib_send.at[0])
    drain(code_own, sib_send.at[1])
    drain(weights.at[:TILE], sib_send.at[2])
    drain(weights.at[:HALF], sib_send.at[3])
    drain(sol_recv, sib_send.at[4])
    drain(base.at[:, :n_far], base_s)
    drain(codes, code_s)
    drain(products, ring_s)
    drain(back_send, back_s)
    drain(block_recv.at[:2 * CHIPS - 1], red_s)


def body(*arrays):
    right_side = arrays[0]
    rows, width = right_side.shape
    dma = pltpu.SemaphoreType.DMA
    any_spec = pl.BlockSpec(memory_space=pl.ANY)
    hbm_spec = pl.BlockSpec(memory_space=pltpu.HBM)
    vmem = pl.BlockSpec(memory_space=pltpu.VMEM)
    out = pltpu.VMEM((rows, width), F32)
    return pl.pallas_call(
        kernel,
        out_shape=(out, out),
        in_specs=[any_spec] * 5 + [hbm_spec] * 3,
        out_specs=(vmem, vmem),
        scratch_shapes=[
            pltpu.SMEM(arrays[5].shape, jnp.int32),
            pltpu.SMEM(arrays[6].shape, jnp.int32),
            pltpu.SMEM(arrays[7].shape, jnp.int32),
            pltpu.SMEM((2 * CHIPS,), jnp.int32),
            pltpu.VMEM((rows, width), BF16),
            pltpu.VMEM((rows, PW), F32),
            pltpu.VMEM((rows, 2 * PW), F32),
            pltpu.VMEM((3 * TILE, W), BF16),
            pltpu.VMEM((CHIPS, 3 * TILE, LANES), BF16),
            pltpu.VMEM((3 * TILE, 2 * W), BF16),
            pltpu.VMEM((TICKS, CHIPS, TILE, LANES), BF16),
            pltpu.VMEM((TICKS, HALF, LANES), BF16),
            pltpu.VMEM((TICKS - 1, 2, CHIPS, TILE, LANES), BF16),
            pltpu.VMEM((TICKS - 1, 2, TILE, LANES), BF16),
            pltpu.VMEM((2 * TILE, LANES), F32),
            pltpu.VMEM((8, LANES), jnp.int32),
            pltpu.VMEM((8, LANES), jnp.int32),
            pltpu.VMEM((8, LANES), jnp.int32),
            pltpu.VMEM((CHIPS, 8, LANES), jnp.int32),
            pltpu.VMEM((TICKS, TILE, LANES), F32),
            pltpu.VMEM((TICKS, HALF, LANES), F32),
            pltpu.VMEM((TICKS - 1, TILE, LANES), F32),
            pltpu.VMEM((TICKS - 1, 2, HALF, LANES), F32),
            pltpu.VMEM((CHIPS, TILE, LANES), BF16),
            pltpu.VMEM((2 * CHIPS, HALF, LANES), BF16),
            dma((8,)), dma((5,)), dma((7,)),
            dma, dma((TICKS, 2)), dma, dma((2,)),
            dma, dma((2, 2, SIDE + 2)), dma, dma, dma, dma,
            pltpu.SemaphoreType.REGULAR,
        ],
        compiler_params=pltpu.CompilerParams(collective_id=0, has_side_effects=True),
        name="chain_solve",
    )(*arrays)


def solution(mesh):
    placed = (
        P(("chain", "rows"), None),
        P(("chain", "rows"), None),
        P("rows", None),
        P("chain", "rows", None),
        P("chain", "rows", None, None),
        P("chain", "rows"),
        P("chain", None),
        P("chain"),
    )
    return jax.shard_map(
        body,
        mesh=mesh,
        in_specs=placed,
        out_specs=(P(("chain", "rows"), None), P(("chain", "rows"), None)),
        check_vma=False,
    )
```

```python
import jax
import jax.numpy as jnp
from jax import lax
from jax.experimental import pallas as pl
from jax.experimental.pallas import tpu as pltpu
from jax.sharding import PartitionSpec as P

PW = 256
TILE = 128
HALF = 64
W = 2048
NZ = 8
SIDE = 4
CHIPS = SIDE * SIDE
TICKS = 3
LANES = 128
F32 = jnp.float32
BF16 = jnp.bfloat16
MESH = pl.DeviceIdType.MESH
HOPS = (1, 3, 2)
RING = (0,) + HOPS
FAR_FIRST = tuple((a, b) for a in range(SIDE - 1, -1, -1) for b in range(SIDE - 1, -1, -1) if (a, b) != (0, 0))
NODES = tuple((f, e) for e in RING for f in range(SIDE))
ROOTS = ((0, 0), (1, 0), (3, 0), (2, 0))
EVENTS = tuple(((f, 0), tuple((f, e) for e in HOPS)) for f in RING)
CHUNK = 8


def slot(f, e):
    return NODES.index((f, e))


def kernel(
    right_side, entering, first_updates, diag_inverse, tile_blocks, targets_in, order_in, count_in,
    sol_out, upd_out,
    targets, order, count, code_table,
    given, enter, first, weights, blocks, placed, base, other_base, products, own_products, acc,
    code_own, code_sib, code_send, codes, sol_send, sol_recv, back_send, back_recv,
    block_send, block_recv,
    load_sem, sib_send, sib_recv, base_s, base_r, code_s, code_r,
    ring_s, ring_r, back_s, back_r, red_s, red_r, last_in,
):
    s = lax.axis_index("chain")
    row = lax.axis_index("rows")
    core = lax.rem(row, 2)
    chip = row // 2
    x = lax.rem(chip, SIDE)
    y = chip // SIDE
    p1 = x + core * (y - x)
    p2 = y + core * (x - y)
    stride1 = 1 + 3 * core
    stride2 = 4 - 3 * core
    up = lax.rem(s + 1, NZ)
    down = lax.rem(s + NZ - 1, NZ)
    sibling = (s, row + 1 - 2 * core)

    def chip_at(d1, d2):
        return lax.rem(p1 + d1 + SIDE, SIDE) * stride1 + lax.rem(p2 + d2 + SIDE, SIDE) * stride2

    def at(plane, d1, d2):
        return (plane, chip_at(d1, d2) * 2 + core)

    def across(plane, d1, d2):
        return (plane, chip_at(d1, d2) * 2 + 1 - core)

    def remote(src, dst, ssem, rsem, device):
        return pltpu.make_async_remote_copy(
            src_ref=src, dst_ref=dst, send_sem=ssem, recv_sem=rsem,
            device_id=device, device_id_type=MESH,
        )

    def drain(ref, sem):
        pltpu.make_async_copy(ref, ref, sem).wait()

    barrier = pltpu.get_barrier_semaphore()

    def greet(device):
        pl.semaphore_signal(barrier, inc=1, device_id=device, device_id_type=MESH)

    greet(sibling)
    for a, b in FAR_FIRST:
        greet(at(s, a, b))
        greet(across(s, a, b))
    in_plane = 1 + 2 * len(FAR_FIRST)
    z_moves = [(f, 0) for f, _ in ROOTS] + [(0, f) for f, _ in ROOTS if f]
    in_z = len(z_moves) + 1
    for a, b in z_moves:
        greet(at(down, SIDE - a, SIDE - b))
    greet(across(down, 0, 0))

    @pl.when(s < NZ - 1)
    def _():
        for a, b in z_moves:
            greet(at(up, a, b))
        greet(across(up, 0, 0))

    my_rows = pl.ds(pl.multiple_of(core * HALF, HALF), HALF)
    their_rows = pl.ds(pl.multiple_of((1 - core) * HALF, HALF), HALF)
    tile_rows = pl.ds(pl.multiple_of(core * TILE, TILE), TILE)
    diag_rows = pl.ds(pl.multiple_of(2 * TILE + core * HALF, HALF), HALF)
    loads = [
        pltpu.make_async_copy(right_side, given, load_sem.at[0]),
        pltpu.make_async_copy(entering, enter, load_sem.at[1]),
        pltpu.make_async_copy(first_updates, first, load_sem.at[2]),
        pltpu.make_async_copy(targets_in, targets, load_sem.at[3]),
        pltpu.make_async_copy(order_in, order, load_sem.at[4]),
        pltpu.make_async_copy(count_in, count, load_sem.at[5]),
        pltpu.make_async_copy(tile_blocks.at[0, 0], weights.at[tile_rows], load_sem.at[6]),
        pltpu.make_async_copy(diag_inverse.at[0], weights.at[diag_rows], load_sem.at[7]),
    ]
    for copy in loads:
        copy.start()
    for copy in loads[:3]:
        copy.wait()
    is_first = (s == 0).astype(F32)

    def head_part(tick, half):
        lanes = pl.ds(pl.multiple_of(tick * PW + half * LANES, LANES), LANES)
        value = given[:, lanes].astype(F32)
        if tick == 0:
            taken = enter[:, pl.ds(pl.multiple_of(half * LANES, LANES), LANES)]
        else:
            lanes = pl.ds(pl.multiple_of((tick - 1) * PW + half * LANES, LANES), LANES)
            taken = is_first * first[:, lanes]
        return (value - taken).astype(BF16)

    for tick in range(TICKS):
        other_base[tick] = head_part(tick, 1 - core)
        base[tick, chip, my_rows] = head_part(tick, core)

    for copy in loads[3:6]:
        copy.wait()
    live = jnp.int32(0)
    for k in range(order.shape[1]):
        hit = jnp.logical_and(order[0, k] == row, k < count[0])
        live = live + hit.astype(jnp.int32)
    code = targets[0, 0] + CHIPS * (1 - live)
    code_rows = lax.broadcasted_iota(jnp.int32, (8, LANES), 0)
    code_own[...] = jnp.where(code_rows == core, code, 0)

    pl.semaphore_wait(barrier, in_plane + in_z + in_z * (s > 0).astype(jnp.int32))

    @pl.when(s == NZ - 1)
    def _():
        for device in (at(up, 0, 0), across(up, 0, 0)):
            pl.semaphore_signal(last_in, inc=1, device_id=device, device_id_type=MESH)

    def sib_base(tick):
        return remote(
            other_base.at[tick], base.at[tick, chip, my_rows],
            sib_send.at[0], sib_recv.at[tick], sibling,
        )

    def sib_code():
        return remote(code_own, code_sib, sib_send.at[1], sib_recv.at[3], sibling)

    def sib_tile():
        return remote(tile_blocks.at[0, 0], weights.at[tile_rows], sib_send.at[2], sib_recv.at[4], sibling)

    def sib_diag():
        return remote(diag_inverse.at[0], weights.at[diag_rows], sib_send.at[3], sib_recv.at[5], sibling)

    def base_half(rows, d1, d2):
        return remote(
            base.at[0, chip, rows], base.at[0, chip, rows],
            base_s, base_r.at[0, 0], at(s, d1, d2),
        )

    n_far = len(FAR_FIRST)
    def base_copy(tick, node, child):
        held = chip_at(-node[0], -node[1])
        return remote(
            base.at[tick, held], base.at[tick, held], base_s, base_r.at[tick, int(child[1] > 0)],
            at(s, child[0] - node[0], child[1] - node[1]),
        )

    def base_along(tick):
        sib_base(tick).wait_recv()
        for f in HOPS:
            base_copy(tick, (0, 0), (f, 0)).start()

    def base_over(tick, rings=RING):
        if rings[0] == 0:
            drain(base.at[tick, :SIDE - 1], base_r.at[tick, 0])
        for f in rings:
            for e in HOPS:
                base_copy(tick, (f, 0), (f, e)).start()

    def base_done(tick):
        drain(base.at[tick, :CHIPS - SIDE], base_r.at[tick, 1])

    sib_base(0).start()
    sib_base(1).start()
    sib_code().start()
    for a, b in FAR_FIRST:
        base_half(my_rows, a, b).start()
    sib_base(0).wait_recv()
    sib_base(1).wait_recv()
    for f in HOPS:
        base_copy(1, (0, 0), (f, 0)).start()
    for a, b in FAR_FIRST:
        base_half(their_rows, b, a).start()
    sib_base(2).start()

    def code_root(f, e):
        return remote(code_send, codes.at[slot(f, e)], code_s, code_r.at[0], at(up, f, e))

    def code_edge(node, child):
        n, m = slot(*node), slot(*child)
        return remote(
            codes.at[n], codes.at[m], code_s, code_r.at[1],
            at(s, child[0] - node[0], child[1] - node[1]),
        )

    sib_code().wait_recv()
    code_send[...] = code_own[...] + code_sib[...]

    for f, e in ROOTS:
        code_root(f, e).start()

    sib_tile().start()
    sib_diag().start()

    base_along(2)
    for copy in loads[6:]:
        copy.wait()
    sib_tile().wait_recv()
    sib_diag().wait_recv()
    for b in range(CHIPS):
        blocks[b] = weights[:, b * TILE:(b + 1) * TILE]

    def pass_codes():
        drain(codes.at[:SIDE], code_r.at[0])
        for node, children in EVENTS:
            for child in children:
                code_edge(node, child).start()


    base_over(1, RING)
    drain(base.at[0, :n_far], base_r.at[0, 0])

    def dot(a, b):
        return jnp.dot(a, b, preferred_element_type=F32)

    def base_rows(tick):
        return base[tick].reshape(W, LANES)

    TOP = slice(0, 2 * TILE)
    LOW = slice(2 * TILE, 3 * TILE)
    def placed_dot(rows, tick, k, part):
        first_slot = part * CHUNK
        col = (k * CHIPS + first_slot) * TILE
        right = products[tick, k, first_slot:first_slot + CHUNK].reshape(CHUNK * TILE, LANES)
        return dot(placed[rows, col:col + CHUNK * TILE], right)

    def move(k, f, e):
        return (f, e) if k == 0 else (e, f)

    def root(tick, k, node):
        n = slot(*node)
        return remote(
            own_products.at[tick, k], products.at[tick, k, n],
            ring_s, ring_r.at[tick, k, n], at(up, *move(k, *node)),
        )

    def edge(tick, k, node, child):
        n, m = slot(*node), slot(*child)
        return remote(
            products.at[tick, k, n], products.at[tick, k, m],
            ring_s, ring_r.at[tick, k, m if m < SIDE else SIDE + m // CHUNK],
            at(s, *move(k, child[0] - node[0], child[1] - node[1])),
        )

    def parts_in(tick, k, part):
        drain(products.at[tick, k, max(part * CHUNK, SIDE):(part + 1) * CHUNK], ring_r.at[tick, k, SIDE + part])

    def pass_on(tick):
        for j, (node, children) in enumerate(EVENTS):
            for k in range(2):
                drain(products.at[tick, k, slot(*node)], ring_r.at[tick, k, slot(*node)])
                for child in children:
                    edge(tick, k, node, child).start()

    def take_products(tick):
        for part in range(2):
            for k in range(2):
                parts_in(tick, k, part)
                acc[...] = acc[...] - placed_dot(TOP, tick, k, part)

    def give_back(tick):
        total = jnp.zeros((TILE, LANES), F32)
        for k in range(2):
            for n in range(CHIPS):
                part = products[tick, k, n].astype(F32)
                total = total + (code_table[k * CHIPS + n] == chip).astype(F32) * part
        back_send[tick] = total
        for h in range(2):
            back(tick, h, core).start()

    def back(tick, h, k):
        return remote(
            back_send.at[tick, h * HALF:(h + 1) * HALF], back_recv.at[tick, k],
            back_s, back_r, (down, chip * 2 + h),
        )

    code_both = [jnp.max(code_send[k:k + 1, :]) for k in range(2)]

    def own_half(n, a, b):
        return remote(
            block_send.at[n, my_rows], block_recv.at[core * CHIPS + n],
            red_s, red_r, at(s, a, b),
        )

    def other_half(n, a, b):
        return remote(
            block_send.at[n, their_rows], block_recv.at[core * CHIPS + n],
            red_s, red_r, across(s, a, b),
        )

    def reduce_out(tick):
        def reduced(target):
            m0 = (code_both[0] == target).astype(F32)
            m1 = (code_both[1] == target).astype(F32)
            return (m0 * acc[:TILE] + m1 * acc[TILE:]).astype(BF16)

        for n, (a, b) in enumerate(FAR_FIRST):
            block_send[n] = reduced(chip_at(a, b))
            own_half(n, a, b).start()
        block_send[n_far] = reduced(chip)
        other_half(n_far, 0, 0).start()
        for b, a in FAR_FIRST:
            n = FAR_FIRST.index((a, b))
            other_half(n, a, b).start()
        block_recv[core * CHIPS + n_far] = block_send[n_far, my_rows]

    def reduce_in(tick):
        drain(block_recv.at[:2 * CHIPS - 1], red_r)
        for k in range(2):
            total = jnp.zeros((HALF, LANES), F32)
            for n in range(CHIPS):
                total = total + block_recv[k * CHIPS + n].astype(F32)
            upd_out[:, tick * PW + k * LANES:tick * PW + (k + 1) * LANES] = total

    def sib_sol(tick):
        return remote(
            sol_send.at[tick, their_rows], sol_recv.at[tick],
            sib_send.at[4], sib_recv.at[6], sibling,
        )

    inner = s > 0

    def read_codes(place):
        drain(codes.at[SIDE:], code_r.at[1])
        for k in range(2):
            for n, (f, e) in enumerate(NODES):
                value = jnp.max(codes[slot(*move(k, f, e)), k:k + 1, :])
                code_table[k * CHIPS + n] = value
                if place:
                    block = lax.rem(value, CHIPS)
                    used = jnp.full((1, LANES), (value < CHIPS).astype(F32)).astype(BF16)
                    col = (k * CHIPS + n) * TILE
                    placed[:, col:col + TILE] = blocks[block] * used

    for tick in range(TICKS):
        if tick:
            base_done(tick)
        acc[...] = dot(weights[TOP], base_rows(tick))
        if tick:
            @pl.when(inner)
            def _():
                take_products(tick - 1)
        if tick == 1:
            @pl.when(s == 0)
            def _():
                pass_codes()
                pass_on(0)
        if tick < TICKS - 1:
            for k in range(2):
                own_products[tick, k] = acc[k * TILE:(k + 1) * TILE].astype(BF16)
            for node in ROOTS:
                for k in range(2):
                    root(tick, k, node).start()
        else:
            reduce_out(tick)
        if tick == 0:
            @pl.when(inner)
            def _():
                pass_codes()
        sol_send[tick] = dot(weights[LOW], base_rows(tick))
        if tick:
            @pl.when(inner)
            def _():
                for k in range(2):
                    for part in range(2):
                        sol_send[tick] = sol_send[tick] - placed_dot(LOW, tick - 1, k, part)
                give_back(tick - 1)
        lanes = pl.ds(pl.multiple_of(tick * PW + core * LANES, LANES), LANES)
        sol_out[:, lanes] = sol_send[tick, my_rows]
        sib_sol(tick).start()
        if tick < TICKS - 1:
            @pl.when(inner)
            def _():
                pass_on(tick)
        if tick == 0:
            base_over(2, RING)
        if tick == 0:
            @pl.when(inner)
            def _():
                read_codes(True)

    @pl.when(s == 0)
    def _():
        read_codes(False)
        pl.semaphore_wait(last_in, 2)
        for tick in range(TICKS - 1):
            if tick:
                pass_on(tick)
            for k in range(2):
                for part in range(2):
                    parts_in(tick, k, part)
            give_back(tick)

    drain(back_recv, back_r)
    for tick in range(TICKS - 1):
        for k in range(2):
            upd_out[:, tick * PW + k * LANES:tick * PW + (k + 1) * LANES] = back_recv[tick, k]
    drain(sol_recv, sib_recv.at[6])
    for tick in range(TICKS):
        lanes = pl.ds(pl.multiple_of(tick * PW + (1 - core) * LANES, LANES), LANES)
        sol_out[:, lanes] = sol_recv[tick]
    reduce_in(TICKS - 1)
    drain(other_base, sib_send.at[0])
    drain(code_own, sib_send.at[1])
    drain(weights.at[:TILE], sib_send.at[2])
    drain(weights.at[:HALF], sib_send.at[3])
    drain(sol_recv, sib_send.at[4])
    drain(base.at[:, :n_far], base_s)
    drain(codes, code_s)
    drain(products, ring_s)
    drain(back_send, back_s)
    drain(block_recv.at[:2 * CHIPS - 1], red_s)


def body(*arrays):
    right_side = arrays[0]
    rows, width = right_side.shape
    dma = pltpu.SemaphoreType.DMA
    any_spec = pl.BlockSpec(memory_space=pl.ANY)
    hbm_spec = pl.BlockSpec(memory_space=pltpu.HBM)
    vmem = pl.BlockSpec(memory_space=pltpu.VMEM)
    out = pltpu.VMEM((rows, width), F32)
    return pl.pallas_call(
        kernel,
        out_shape=(out, out),
        in_specs=[any_spec] * 5 + [hbm_spec] * 3,
        out_specs=(vmem, vmem),
        scratch_shapes=[
            pltpu.SMEM(arrays[5].shape, jnp.int32),
            pltpu.SMEM(arrays[6].shape, jnp.int32),
            pltpu.SMEM(arrays[7].shape, jnp.int32),
            pltpu.SMEM((2 * CHIPS,), jnp.int32),
            pltpu.VMEM((rows, width), BF16),
            pltpu.VMEM((rows, PW), F32),
            pltpu.VMEM((rows, 2 * PW), F32),
            pltpu.VMEM((3 * TILE, W), BF16),
            pltpu.VMEM((CHIPS, 3 * TILE, LANES), BF16),
            pltpu.VMEM((3 * TILE, 2 * W), BF16),
            pltpu.VMEM((TICKS, CHIPS, TILE, LANES), BF16),
            pltpu.VMEM((TICKS, HALF, LANES), BF16),
            pltpu.VMEM((TICKS - 1, 2, CHIPS, TILE, LANES), BF16),
            pltpu.VMEM((TICKS - 1, 2, TILE, LANES), BF16),
            pltpu.VMEM((2 * TILE, LANES), F32),
            pltpu.VMEM((8, LANES), jnp.int32),
            pltpu.VMEM((8, LANES), jnp.int32),
            pltpu.VMEM((8, LANES), jnp.int32),
            pltpu.VMEM((CHIPS, 8, LANES), jnp.int32),
            pltpu.VMEM((TICKS, TILE, LANES), F32),
            pltpu.VMEM((TICKS, HALF, LANES), F32),
            pltpu.VMEM((TICKS - 1, TILE, LANES), F32),
            pltpu.VMEM((TICKS - 1, 2, HALF, LANES), F32),
            pltpu.VMEM((CHIPS, TILE, LANES), BF16),
            pltpu.VMEM((2 * CHIPS, HALF, LANES), BF16),
            dma((8,)), dma((5,)), dma((7,)),
            dma, dma((TICKS, 2)), dma, dma((2,)),
            dma, dma((2, 2, SIDE + 2)), dma, dma, dma, dma,
            pltpu.SemaphoreType.REGULAR,
        ],
        compiler_params=pltpu.CompilerParams(collective_id=0, has_side_effects=True),
        name="chain_solve",
    )(*arrays)


def solution(mesh):
    placed = (
        P(("chain", "rows"), None),
        P(("chain", "rows"), None),
        P("rows", None),
        P("chain", "rows", None),
        P("chain", "rows", None, None),
        P("chain", "rows"),
        P("chain", None),
        P("chain"),
    )
    return jax.shard_map(
        body,
        mesh=mesh,
        in_specs=placed,
        out_specs=(P(("chain", "rows"), None), P(("chain", "rows"), None)),
        check_vma=False,
    )
```

```python
import jax
import jax.numpy as jnp
from jax import lax
from jax.experimental import pallas as pl
from jax.experimental.pallas import tpu as pltpu
from jax.sharding import PartitionSpec as P

PW = 256
TILE = 128
HALF = 64
W = 2048
NZ = 8
SIDE = 4
CHIPS = SIDE * SIDE
TICKS = 3
LANES = 128
F32 = jnp.float32
BF16 = jnp.bfloat16
MESH = pl.DeviceIdType.MESH
HOPS = (1, 3, 2)
RING = (0,) + HOPS
FAR_FIRST = tuple((a, b) for a in range(SIDE - 1, -1, -1) for b in range(SIDE - 1, -1, -1) if (a, b) != (0, 0))
NODES = tuple((f, e) for e in RING for f in range(SIDE))
ROOTS = ((0, 0), (1, 0), (3, 0), (2, 0))
EVENTS = tuple(((f, 0), tuple((f, e) for e in HOPS)) for f in RING)
CHUNK = 8


def slot(f, e):
    return NODES.index((f, e))


def kernel(
    right_side, entering, first_updates, diag_inverse, tile_blocks, targets_in, order_in, count_in,
    both_out,
    targets, order, count, code_table,
    given, enter, first, weights, blocks, placed, base, other_base, products, own_products, acc,
    code_own, code_sib, code_send, codes, sol_send, sol_recv, back_send, back_recv,
    block_send, block_recv,
    load_sem, sib_send, sib_recv, base_s, base_r, code_s, code_r,
    ring_s, ring_r, back_s, back_r, red_s, red_r, last_in,
):
    rows_out = both_out.shape[0] // 2
    sol_out, upd_out = both_out.at[:rows_out], both_out.at[rows_out:]
    s = lax.axis_index("chain")
    row = lax.axis_index("rows")
    core = lax.rem(row, 2)
    chip = row // 2
    x = lax.rem(chip, SIDE)
    y = chip // SIDE
    p1 = x + core * (y - x)
    p2 = y + core * (x - y)
    stride1 = 1 + 3 * core
    stride2 = 4 - 3 * core
    up = lax.rem(s + 1, NZ)
    down = lax.rem(s + NZ - 1, NZ)
    sibling = (s, row + 1 - 2 * core)

    def chip_at(d1, d2):
        return lax.rem(p1 + d1 + SIDE, SIDE) * stride1 + lax.rem(p2 + d2 + SIDE, SIDE) * stride2

    def at(plane, d1, d2):
        return (plane, chip_at(d1, d2) * 2 + core)

    def across(plane, d1, d2):
        return (plane, chip_at(d1, d2) * 2 + 1 - core)

    def remote(src, dst, ssem, rsem, device):
        return pltpu.make_async_remote_copy(
            src_ref=src, dst_ref=dst, send_sem=ssem, recv_sem=rsem,
            device_id=device, device_id_type=MESH,
        )

    def drain(ref, sem):
        pltpu.make_async_copy(ref, ref, sem).wait()

    barrier = pltpu.get_barrier_semaphore()

    def greet(device):
        pl.semaphore_signal(barrier, inc=1, device_id=device, device_id_type=MESH)

    greet(sibling)
    for a, b in FAR_FIRST:
        greet(at(s, a, b))
        greet(across(s, a, b))
    in_plane = 1 + 2 * len(FAR_FIRST)
    z_moves = [(f, 0) for f, _ in ROOTS] + [(0, f) for f, _ in ROOTS if f]
    in_z = len(z_moves) + 1
    for a, b in z_moves:
        greet(at(down, SIDE - a, SIDE - b))
    greet(across(down, 0, 0))

    @pl.when(s < NZ - 1)
    def _():
        for a, b in z_moves:
            greet(at(up, a, b))
        greet(across(up, 0, 0))

    my_rows = pl.ds(pl.multiple_of(core * HALF, HALF), HALF)
    their_rows = pl.ds(pl.multiple_of((1 - core) * HALF, HALF), HALF)
    tile_rows = pl.ds(pl.multiple_of(core * TILE, TILE), TILE)
    diag_rows = pl.ds(pl.multiple_of(2 * TILE + core * HALF, HALF), HALF)
    loads = [
        pltpu.make_async_copy(right_side, given, load_sem.at[0]),
        pltpu.make_async_copy(entering, enter, load_sem.at[1]),
        pltpu.make_async_copy(first_updates, first, load_sem.at[2]),
        pltpu.make_async_copy(targets_in, targets, load_sem.at[3]),
        pltpu.make_async_copy(order_in, order, load_sem.at[4]),
        pltpu.make_async_copy(count_in, count, load_sem.at[5]),
        pltpu.make_async_copy(tile_blocks.at[0, 0], weights.at[tile_rows], load_sem.at[6]),
        pltpu.make_async_copy(diag_inverse.at[0], weights.at[diag_rows], load_sem.at[7]),
    ]
    for copy in loads:
        copy.start()
    for copy in loads[:3]:
        copy.wait()
    is_first = (s == 0).astype(F32)

    def head_part(tick, half):
        lanes = pl.ds(pl.multiple_of(tick * PW + half * LANES, LANES), LANES)
        value = given[:, lanes].astype(F32)
        if tick == 0:
            taken = enter[:, pl.ds(pl.multiple_of(half * LANES, LANES), LANES)]
        else:
            lanes = pl.ds(pl.multiple_of((tick - 1) * PW + half * LANES, LANES), LANES)
            taken = is_first * first[:, lanes]
        return (value - taken).astype(BF16)

    for tick in range(TICKS):
        other_base[tick] = head_part(tick, 1 - core)
        base[tick, chip, my_rows] = head_part(tick, core)

    for copy in loads[3:6]:
        copy.wait()
    live = jnp.int32(0)
    for k in range(order.shape[1]):
        hit = jnp.logical_and(order[0, k] == row, k < count[0])
        live = live + hit.astype(jnp.int32)
    code = targets[0, 0] + CHIPS * (1 - live)
    code_rows = lax.broadcasted_iota(jnp.int32, (8, LANES), 0)
    code_own[...] = jnp.where(code_rows == core, code, 0)

    pl.semaphore_wait(barrier, in_plane + in_z + in_z * (s > 0).astype(jnp.int32))

    @pl.when(s == NZ - 1)
    def _():
        for device in (at(up, 0, 0), across(up, 0, 0)):
            pl.semaphore_signal(last_in, inc=1, device_id=device, device_id_type=MESH)

    def sib_base(tick):
        return remote(
            other_base.at[tick], base.at[tick, chip, my_rows],
            sib_send.at[0], sib_recv.at[tick], sibling,
        )

    def sib_code():
        return remote(code_own, code_sib, sib_send.at[1], sib_recv.at[3], sibling)

    def sib_tile():
        return remote(tile_blocks.at[0, 0], weights.at[tile_rows], sib_send.at[2], sib_recv.at[4], sibling)

    def sib_diag():
        return remote(diag_inverse.at[0], weights.at[diag_rows], sib_send.at[3], sib_recv.at[5], sibling)

    def base_half(rows, d1, d2):
        return remote(
            base.at[0, chip, rows], base.at[0, chip, rows],
            base_s, base_r.at[0, 0], at(s, d1, d2),
        )

    n_far = len(FAR_FIRST)
    def base_copy(tick, node, child):
        held = chip_at(-node[0], -node[1])
        return remote(
            base.at[tick, held], base.at[tick, held], base_s, base_r.at[tick, int(child[1] > 0)],
            at(s, child[0] - node[0], child[1] - node[1]),
        )

    def base_along(tick):
        sib_base(tick).wait_recv()
        for f in HOPS:
            base_copy(tick, (0, 0), (f, 0)).start()

    def base_over(tick, rings=RING):
        if rings[0] == 0:
            drain(base.at[tick, :SIDE - 1], base_r.at[tick, 0])
        for f in rings:
            for e in HOPS:
                base_copy(tick, (f, 0), (f, e)).start()

    def base_done(tick):
        drain(base.at[tick, :CHIPS - SIDE], base_r.at[tick, 1])

    sib_base(0).start()
    sib_base(1).start()
    sib_code().start()
    for a, b in FAR_FIRST:
        base_half(my_rows, a, b).start()
    sib_base(0).wait_recv()
    sib_base(1).wait_recv()
    for f in HOPS:
        base_copy(1, (0, 0), (f, 0)).start()
    for a, b in FAR_FIRST:
        base_half(their_rows, b, a).start()
    sib_base(2).start()

    def code_root(f, e):
        return remote(code_send, codes.at[slot(f, e)], code_s, code_r.at[0], at(up, f, e))

    def code_edge(node, child):
        n, m = slot(*node), slot(*child)
        return remote(
            codes.at[n], codes.at[m], code_s, code_r.at[1],
            at(s, child[0] - node[0], child[1] - node[1]),
        )

    sib_code().wait_recv()
    code_send[...] = code_own[...] + code_sib[...]

    for f, e in ROOTS:
        code_root(f, e).start()

    sib_tile().start()
    sib_diag().start()

    base_along(2)
    for copy in loads[6:]:
        copy.wait()
    sib_tile().wait_recv()
    sib_diag().wait_recv()
    for b in range(CHIPS):
        blocks[b] = weights[:, b * TILE:(b + 1) * TILE]

    def pass_codes():
        drain(codes.at[:SIDE], code_r.at[0])
        for node, children in EVENTS:
            for child in children:
                code_edge(node, child).start()


    base_over(1, RING)
    drain(base.at[0, :n_far], base_r.at[0, 0])

    def dot(a, b):
        return jnp.dot(a, b, preferred_element_type=F32)

    def base_rows(tick):
        return base[tick].reshape(W, LANES)

    TOP = slice(0, 2 * TILE)
    LOW = slice(2 * TILE, 3 * TILE)
    def placed_dot(rows, tick, k, part):
        first_slot = part * CHUNK
        col = (k * CHIPS + first_slot) * TILE
        right = products[tick, k, first_slot:first_slot + CHUNK].reshape(CHUNK * TILE, LANES)
        return dot(placed[rows, col:col + CHUNK * TILE], right)

    def move(k, f, e):
        return (f, e) if k == 0 else (e, f)

    def root(tick, k, node):
        n = slot(*node)
        return remote(
            own_products.at[tick, k], products.at[tick, k, n],
            ring_s, ring_r.at[tick, k, n], at(up, *move(k, *node)),
        )

    def edge(tick, k, node, child):
        n, m = slot(*node), slot(*child)
        return remote(
            products.at[tick, k, n], products.at[tick, k, m],
            ring_s, ring_r.at[tick, k, m if m < SIDE else SIDE + m // CHUNK],
            at(s, *move(k, child[0] - node[0], child[1] - node[1])),
        )

    def parts_in(tick, k, part):
        drain(products.at[tick, k, max(part * CHUNK, SIDE):(part + 1) * CHUNK], ring_r.at[tick, k, SIDE + part])

    def pass_on(tick):
        for j, (node, children) in enumerate(EVENTS):
            for k in range(2):
                drain(products.at[tick, k, slot(*node)], ring_r.at[tick, k, slot(*node)])
                for child in children:
                    edge(tick, k, node, child).start()

    def take_products(tick):
        for part in range(2):
            for k in range(2):
                parts_in(tick, k, part)
                acc[...] = acc[...] - placed_dot(TOP, tick, k, part)

    def give_back(tick):
        total = jnp.zeros((TILE, LANES), F32)
        for k in range(2):
            for n in range(CHIPS):
                part = products[tick, k, n].astype(F32)
                total = total + (code_table[k * CHIPS + n] == chip).astype(F32) * part
        back_send[tick] = total
        for h in range(2):
            back(tick, h, core).start()

    def back(tick, h, k):
        return remote(
            back_send.at[tick, h * HALF:(h + 1) * HALF], back_recv.at[tick, k],
            back_s, back_r, (down, chip * 2 + h),
        )

    code_both = [jnp.max(code_send[k:k + 1, :]) for k in range(2)]

    def own_half(n, a, b):
        return remote(
            block_send.at[n, my_rows], block_recv.at[core * CHIPS + n],
            red_s, red_r, at(s, a, b),
        )

    def other_half(n, a, b):
        return remote(
            block_send.at[n, their_rows], block_recv.at[core * CHIPS + n],
            red_s, red_r, across(s, a, b),
        )

    def reduce_out(tick):
        def reduced(target):
            m0 = (code_both[0] == target).astype(F32)
            m1 = (code_both[1] == target).astype(F32)
            return (m0 * acc[:TILE] + m1 * acc[TILE:]).astype(BF16)

        for n, (a, b) in enumerate(FAR_FIRST):
            block_send[n] = reduced(chip_at(a, b))
            own_half(n, a, b).start()
        block_send[n_far] = reduced(chip)
        other_half(n_far, 0, 0).start()
        for b, a in FAR_FIRST:
            n = FAR_FIRST.index((a, b))
            other_half(n, a, b).start()
        block_recv[core * CHIPS + n_far] = block_send[n_far, my_rows]

    def reduce_in(tick):
        drain(block_recv.at[:2 * CHIPS - 1], red_r)
        for k in range(2):
            total = jnp.zeros((HALF, LANES), F32)
            for n in range(CHIPS):
                total = total + block_recv[k * CHIPS + n].astype(F32)
            upd_out[:, tick * PW + k * LANES:tick * PW + (k + 1) * LANES] = total

    def sib_sol(tick):
        return remote(
            sol_send.at[tick, their_rows], sol_recv.at[tick],
            sib_send.at[4], sib_recv.at[6], sibling,
        )

    inner = s > 0

    def read_codes(place):
        drain(codes.at[SIDE:], code_r.at[1])
        for k in range(2):
            for n, (f, e) in enumerate(NODES):
                value = jnp.max(codes[slot(*move(k, f, e)), k:k + 1, :])
                code_table[k * CHIPS + n] = value
                if place:
                    block = lax.rem(value, CHIPS)
                    used = jnp.full((1, LANES), (value < CHIPS).astype(F32)).astype(BF16)
                    col = (k * CHIPS + n) * TILE
                    placed[:, col:col + TILE] = blocks[block] * used

    for tick in range(TICKS):
        if tick:
            base_done(tick)
        acc[...] = dot(weights[TOP], base_rows(tick))
        if tick:
            @pl.when(inner)
            def _():
                take_products(tick - 1)
        if tick == 1:
            @pl.when(s == 0)
            def _():
                pass_codes()
                pass_on(0)
        if tick < TICKS - 1:
            for k in range(2):
                own_products[tick, k] = acc[k * TILE:(k + 1) * TILE].astype(BF16)
            for node in ROOTS:
                for k in range(2):
                    root(tick, k, node).start()
        else:
            reduce_out(tick)
        if tick == 0:
            @pl.when(inner)
            def _():
                pass_codes()
        sol_send[tick] = dot(weights[LOW], base_rows(tick))
        if tick:
            @pl.when(inner)
            def _():
                for k in range(2):
                    for part in range(2):
                        sol_send[tick] = sol_send[tick] - placed_dot(LOW, tick - 1, k, part)
                give_back(tick - 1)
        lanes = pl.ds(pl.multiple_of(tick * PW + core * LANES, LANES), LANES)
        sol_out[:, lanes] = sol_send[tick, my_rows]
        sib_sol(tick).start()
        if tick < TICKS - 1:
            @pl.when(inner)
            def _():
                pass_on(tick)
        if tick == 0:
            base_over(2, RING)
        if tick == 0:
            @pl.when(inner)
            def _():
                read_codes(True)

    @pl.when(s == 0)
    def _():
        read_codes(False)
        pl.semaphore_wait(last_in, 2)
        for tick in range(TICKS - 1):
            if tick:
                pass_on(tick)
            for k in range(2):
                for part in range(2):
                    parts_in(tick, k, part)
            give_back(tick)

    drain(back_recv, back_r)
    for tick in range(TICKS - 1):
        for k in range(2):
            upd_out[:, tick * PW + k * LANES:tick * PW + (k + 1) * LANES] = back_recv[tick, k]
    drain(sol_recv, sib_recv.at[6])
    for tick in range(TICKS):
        lanes = pl.ds(pl.multiple_of(tick * PW + (1 - core) * LANES, LANES), LANES)
        sol_out[:, lanes] = sol_recv[tick]
    reduce_in(TICKS - 1)
    drain(other_base, sib_send.at[0])
    drain(code_own, sib_send.at[1])
    drain(weights.at[:TILE], sib_send.at[2])
    drain(weights.at[:HALF], sib_send.at[3])
    drain(sol_recv, sib_send.at[4])
    drain(base.at[:, :n_far], base_s)
    drain(codes, code_s)
    drain(products, ring_s)
    drain(back_send, back_s)
    drain(block_recv.at[:2 * CHIPS - 1], red_s)


def body(*arrays):
    right_side = arrays[0]
    rows, width = right_side.shape
    dma = pltpu.SemaphoreType.DMA
    any_spec = pl.BlockSpec(memory_space=pl.ANY)
    hbm_spec = pl.BlockSpec(memory_space=pltpu.HBM)
    vmem = pl.BlockSpec(memory_space=pltpu.VMEM)
    out = pltpu.VMEM((2 * rows, width), F32)
    both = pl.pallas_call(
        kernel,
        out_shape=out,
        in_specs=[any_spec] * 5 + [hbm_spec] * 3,
        out_specs=vmem,
        scratch_shapes=[
            pltpu.SMEM(arrays[5].shape, jnp.int32),
            pltpu.SMEM(arrays[6].shape, jnp.int32),
            pltpu.SMEM(arrays[7].shape, jnp.int32),
            pltpu.SMEM((2 * CHIPS,), jnp.int32),
            pltpu.VMEM((rows, width), BF16),
            pltpu.VMEM((rows, PW), F32),
            pltpu.VMEM((rows, 2 * PW), F32),
            pltpu.VMEM((3 * TILE, W), BF16),
            pltpu.VMEM((CHIPS, 3 * TILE, LANES), BF16),
            pltpu.VMEM((3 * TILE, 2 * W), BF16),
            pltpu.VMEM((TICKS, CHIPS, TILE, LANES), BF16),
            pltpu.VMEM((TICKS, HALF, LANES), BF16),
            pltpu.VMEM((TICKS - 1, 2, CHIPS, TILE, LANES), BF16),
            pltpu.VMEM((TICKS - 1, 2, TILE, LANES), BF16),
            pltpu.VMEM((2 * TILE, LANES), F32),
            pltpu.VMEM((8, LANES), jnp.int32),
            pltpu.VMEM((8, LANES), jnp.int32),
            pltpu.VMEM((8, LANES), jnp.int32),
            pltpu.VMEM((CHIPS, 8, LANES), jnp.int32),
            pltpu.VMEM((TICKS, TILE, LANES), F32),
            pltpu.VMEM((TICKS, HALF, LANES), F32),
            pltpu.VMEM((TICKS - 1, TILE, LANES), F32),
            pltpu.VMEM((TICKS - 1, 2, HALF, LANES), F32),
            pltpu.VMEM((CHIPS, TILE, LANES), BF16),
            pltpu.VMEM((2 * CHIPS, HALF, LANES), BF16),
            dma((8,)), dma((5,)), dma((7,)),
            dma, dma((TICKS, 2)), dma, dma((2,)),
            dma, dma((2, 2, SIDE + 2)), dma, dma, dma, dma,
            pltpu.SemaphoreType.REGULAR,
        ],
        compiler_params=pltpu.CompilerParams(collective_id=0, has_side_effects=True),
        name="chain_solve",
    )(*arrays)
    return both[:rows], both[rows:]


def solution(mesh):
    placed = (
        P(("chain", "rows"), None),
        P(("chain", "rows"), None),
        P("rows", None),
        P("chain", "rows", None),
        P("chain", "rows", None, None),
        P("chain", "rows"),
        P("chain", None),
        P("chain"),
    )
    return jax.shard_map(
        body,
        mesh=mesh,
        in_specs=placed,
        out_specs=(P(("chain", "rows"), None), P(("chain", "rows"), None)),
        check_vma=False,
    )
```

```python
import jax
import jax.numpy as jnp
from jax import lax
from jax.experimental import pallas as pl
from jax.experimental.pallas import tpu as pltpu
from jax.sharding import PartitionSpec as P

PW = 256
TILE = 128
HALF = 64
W = 2048
NZ = 8
SIDE = 4
CHIPS = SIDE * SIDE
TICKS = 3
LANES = 128
F32 = jnp.float32
BF16 = jnp.bfloat16
MESH = pl.DeviceIdType.MESH
HOPS = (1, 3, 2)
RING = (0,) + HOPS
FAR_FIRST = tuple((a, b) for a in range(SIDE - 1, -1, -1) for b in range(SIDE - 1, -1, -1) if (a, b) != (0, 0))
NODES = tuple((f, e) for e in RING for f in range(SIDE))
ROOTS = ((0, 0), (1, 0), (3, 0), (2, 0))
EVENTS = tuple(((f, 0), tuple((f, e) for e in HOPS)) for f in RING)
CHUNK = 8


def slot(f, e):
    return NODES.index((f, e))


def kernel(
    right_side, entering, first_updates, diag_inverse, tile_blocks, targets_in, order_in, count_in,
    both_out,
    targets, order, count, code_table,
    given, enter, first, weights, blocks, placed, base, other_base, products, own_products, acc,
    code_own, code_sib, code_send, codes, sol_send, sol_recv, back_send, back_recv,
    block_send, block_recv,
    load_sem, sib_send, sib_recv, base_s, base_r, code_s, code_r,
    ring_s, ring_r, back_s, back_r, red_s, red_r, last_in,
):
    rows_out = both_out.shape[0] // 2
    sol_out, upd_out = both_out.at[:rows_out], both_out.at[rows_out:]
    s = lax.axis_index("chain")
    row = lax.axis_index("rows")
    core = lax.rem(row, 2)
    chip = row // 2
    x = lax.rem(chip, SIDE)
    y = chip // SIDE
    p1 = x + core * (y - x)
    p2 = y + core * (x - y)
    stride1 = 1 + 3 * core
    stride2 = 4 - 3 * core
    up = lax.rem(s + 1, NZ)
    down = lax.rem(s + NZ - 1, NZ)
    sibling = (s, row + 1 - 2 * core)

    def chip_at(d1, d2):
        return lax.rem(p1 + d1 + SIDE, SIDE) * stride1 + lax.rem(p2 + d2 + SIDE, SIDE) * stride2

    def at(plane, d1, d2):
        return (plane, chip_at(d1, d2) * 2 + core)

    def across(plane, d1, d2):
        return (plane, chip_at(d1, d2) * 2 + 1 - core)

    def remote(src, dst, ssem, rsem, device):
        return pltpu.make_async_remote_copy(
            src_ref=src, dst_ref=dst, send_sem=ssem, recv_sem=rsem,
            device_id=device, device_id_type=MESH,
        )

    def drain(ref, sem):
        pltpu.make_async_copy(ref, ref, sem).wait()

    barrier = pltpu.get_barrier_semaphore()

    def greet(device):
        pl.semaphore_signal(barrier, inc=1, device_id=device, device_id_type=MESH)

    greet(sibling)
    for a, b in FAR_FIRST:
        greet(at(s, a, b))
        greet(across(s, a, b))
    in_plane = 1 + 2 * len(FAR_FIRST)
    z_moves = [(f, 0) for f, _ in ROOTS] + [(0, f) for f, _ in ROOTS if f]
    in_z = len(z_moves) + 1
    for a, b in z_moves:
        greet(at(down, SIDE - a, SIDE - b))
    greet(across(down, 0, 0))

    @pl.when(s < NZ - 1)
    def _():
        for a, b in z_moves:
            greet(at(up, a, b))
        greet(across(up, 0, 0))

    my_rows = pl.ds(pl.multiple_of(core * HALF, HALF), HALF)
    their_rows = pl.ds(pl.multiple_of((1 - core) * HALF, HALF), HALF)
    tile_rows = pl.ds(pl.multiple_of(core * TILE, TILE), TILE)
    diag_rows = pl.ds(pl.multiple_of(2 * TILE + core * HALF, HALF), HALF)
    loads = [
        pltpu.make_async_copy(right_side, given, load_sem.at[0]),
        pltpu.make_async_copy(entering, enter, load_sem.at[1]),
        pltpu.make_async_copy(first_updates, first, load_sem.at[2]),
        pltpu.make_async_copy(targets_in, targets, load_sem.at[3]),
        pltpu.make_async_copy(order_in, order, load_sem.at[4]),
        pltpu.make_async_copy(count_in, count, load_sem.at[5]),
        pltpu.make_async_copy(tile_blocks.at[0, 0], weights.at[tile_rows], load_sem.at[6]),
        pltpu.make_async_copy(diag_inverse.at[0], weights.at[diag_rows], load_sem.at[7]),
    ]
    for copy in loads:
        copy.start()
    for copy in loads[:3]:
        copy.wait()
    is_first = (s == 0).astype(F32)

    def head_part(tick, half):
        lanes = pl.ds(pl.multiple_of(tick * PW + half * LANES, LANES), LANES)
        value = given[:, lanes].astype(F32)
        if tick == 0:
            taken = enter[:, pl.ds(pl.multiple_of(half * LANES, LANES), LANES)]
        else:
            lanes = pl.ds(pl.multiple_of((tick - 1) * PW + half * LANES, LANES), LANES)
            taken = is_first * first[:, lanes]
        return (value - taken).astype(BF16)

    for tick in range(TICKS):
        other_base[tick] = head_part(tick, 1 - core)
        base[tick, chip, my_rows] = head_part(tick, core)

    for copy in loads[3:6]:
        copy.wait()
    live = jnp.int32(0)
    for k in range(order.shape[1]):
        hit = jnp.logical_and(order[0, k] == row, k < count[0])
        live = live + hit.astype(jnp.int32)
    code = targets[0, 0] + CHIPS * (1 - live)
    code_rows = lax.broadcasted_iota(jnp.int32, (8, LANES), 0)
    code_own[...] = jnp.where(code_rows == core, code, 0)

    pl.semaphore_wait(barrier, in_plane + in_z + in_z * (s > 0).astype(jnp.int32))

    @pl.when(s == NZ - 1)
    def _():
        for device in (at(up, 0, 0), across(up, 0, 0)):
            pl.semaphore_signal(last_in, inc=1, device_id=device, device_id_type=MESH)

    def sib_base(tick):
        return remote(
            other_base.at[tick], base.at[tick, chip, my_rows],
            sib_send.at[0], sib_recv.at[tick], sibling,
        )

    def sib_code():
        return remote(code_own, code_sib, sib_send.at[1], sib_recv.at[3], sibling)

    def sib_tile():
        return remote(tile_blocks.at[0, 0], weights.at[tile_rows], sib_send.at[2], sib_recv.at[4], sibling)

    def sib_diag():
        return remote(diag_inverse.at[0], weights.at[diag_rows], sib_send.at[3], sib_recv.at[5], sibling)

    def base_half(rows, d1, d2):
        return remote(
            base.at[0, chip, rows], base.at[0, chip, rows],
            base_s, base_r.at[0, 0], at(s, d1, d2),
        )

    n_far = len(FAR_FIRST)
    def base_copy(tick, node, child):
        held = chip_at(-node[0], -node[1])
        return remote(
            base.at[tick, held], base.at[tick, held], base_s, base_r.at[tick, int(child[1] > 0)],
            at(s, child[0] - node[0], child[1] - node[1]),
        )

    def base_along(tick):
        sib_base(tick).wait_recv()
        for f in HOPS:
            base_copy(tick, (0, 0), (f, 0)).start()

    def base_over(tick, rings=RING):
        if rings[0] == 0:
            drain(base.at[tick, :SIDE - 1], base_r.at[tick, 0])
        for f in rings:
            for e in HOPS:
                base_copy(tick, (f, 0), (f, e)).start()

    def base_done(tick):
        drain(base.at[tick, :CHIPS - SIDE], base_r.at[tick, 1])

    sib_base(0).start()
    sib_base(1).start()
    sib_code().start()
    for a, b in FAR_FIRST:
        base_half(my_rows, a, b).start()
    sib_base(0).wait_recv()
    sib_base(1).wait_recv()
    for f in HOPS:
        base_copy(1, (0, 0), (f, 0)).start()
    for a, b in FAR_FIRST:
        base_half(their_rows, b, a).start()
    sib_base(2).start()

    def code_root(f, e):
        return remote(code_send, codes.at[slot(f, e)], code_s, code_r.at[0], at(up, f, e))

    def code_edge(node, child):
        n, m = slot(*node), slot(*child)
        return remote(
            codes.at[n], codes.at[m], code_s, code_r.at[1],
            at(s, child[0] - node[0], child[1] - node[1]),
        )

    sib_code().wait_recv()
    code_send[...] = code_own[...] + code_sib[...]

    for f, e in ROOTS:
        code_root(f, e).start()

    sib_tile().start()
    sib_diag().start()

    base_along(2)
    for copy in loads[6:]:
        copy.wait()
    sib_tile().wait_recv()

    def pass_codes():
        drain(codes.at[:SIDE], code_r.at[0])
        for node, children in EVENTS:
            for child in children:
                code_edge(node, child).start()


    base_over(1, RING)
    drain(base.at[0, :n_far], base_r.at[0, 0])

    def dot(a, b):
        return jnp.dot(a, b, preferred_element_type=F32)

    def base_rows(tick):
        return base[tick].reshape(W, LANES)

    TOP = slice(0, 2 * TILE)
    LOW = slice(2 * TILE, 3 * TILE)
    def placed_dot(rows, tick, k, part):
        first_slot = part * CHUNK
        col = (k * CHIPS + first_slot) * TILE
        right = products[tick, k, first_slot:first_slot + CHUNK].reshape(CHUNK * TILE, LANES)
        return dot(placed[rows, col:col + CHUNK * TILE], right)

    def move(k, f, e):
        return (f, e) if k == 0 else (e, f)

    def root(tick, k, node):
        n = slot(*node)
        return remote(
            own_products.at[tick, k], products.at[tick, k, n],
            ring_s, ring_r.at[tick, k, n], at(up, *move(k, *node)),
        )

    def edge(tick, k, node, child):
        n, m = slot(*node), slot(*child)
        return remote(
            products.at[tick, k, n], products.at[tick, k, m],
            ring_s, ring_r.at[tick, k, m if m < SIDE else SIDE + m // CHUNK],
            at(s, *move(k, child[0] - node[0], child[1] - node[1])),
        )

    def parts_in(tick, k, part):
        drain(products.at[tick, k, max(part * CHUNK, SIDE):(part + 1) * CHUNK], ring_r.at[tick, k, SIDE + part])

    def pass_on(tick):
        for j, (node, children) in enumerate(EVENTS):
            for k in range(2):
                drain(products.at[tick, k, slot(*node)], ring_r.at[tick, k, slot(*node)])
                for child in (children if k == 0 else children[1::-1] + children[2:]):
                    edge(tick, k, node, child).start()

    def take_products(tick):
        for part in range(2):
            for k in range(2):
                parts_in(tick, k, part)
                acc[...] = acc[...] - placed_dot(TOP, tick, k, part)

    def give_back(tick):
        total = jnp.zeros((TILE, LANES), F32)
        for k in range(2):
            for n in range(CHIPS):
                part = products[tick, k, n].astype(F32)
                total = total + (code_table[k * CHIPS + n] == chip).astype(F32) * part
        back_send[tick] = total
        for h in range(2):
            back(tick, h, core).start()

    def back(tick, h, k):
        return remote(
            back_send.at[tick, h * HALF:(h + 1) * HALF], back_recv.at[tick, k],
            back_s, back_r, (down, chip * 2 + h),
        )

    code_both = [jnp.max(code_send[k:k + 1, :]) for k in range(2)]

    def own_half(n, a, b):
        return remote(
            block_send.at[n, my_rows], block_recv.at[core * CHIPS + n],
            red_s, red_r, at(s, a, b),
        )

    def other_half(n, a, b):
        return remote(
            block_send.at[n, their_rows], block_recv.at[core * CHIPS + n],
            red_s, red_r, across(s, a, b),
        )

    def reduce_out(tick):
        def reduced(target):
            m0 = (code_both[0] == target).astype(F32)
            m1 = (code_both[1] == target).astype(F32)
            return (m0 * acc[:TILE] + m1 * acc[TILE:]).astype(BF16)

        for n, (a, b) in enumerate(FAR_FIRST):
            block_send[n] = reduced(chip_at(a, b))
            own_half(n, a, b).start()
        block_send[n_far] = reduced(chip)
        other_half(n_far, 0, 0).start()
        for b, a in FAR_FIRST:
            n = FAR_FIRST.index((a, b))
            other_half(n, a, b).start()
        block_recv[core * CHIPS + n_far] = block_send[n_far, my_rows]

    def reduce_in(tick):
        drain(block_recv.at[:2 * CHIPS - 1], red_r)
        for k in range(2):
            total = jnp.zeros((HALF, LANES), F32)
            for n in range(CHIPS):
                total = total + block_recv[k * CHIPS + n].astype(F32)
            upd_out[:, tick * PW + k * LANES:tick * PW + (k + 1) * LANES] = total

    def sib_sol(tick):
        return remote(
            sol_send.at[tick, their_rows], sol_recv.at[tick],
            sib_send.at[4], sib_recv.at[6], sibling,
        )

    inner = s > 0

    def read_codes(place):
        drain(codes.at[SIDE:], code_r.at[1])
        for k in range(2):
            for n, (f, e) in enumerate(NODES):
                value = jnp.max(codes[slot(*move(k, f, e)), k:k + 1, :])
                code_table[k * CHIPS + n] = value
                if place:
                    block = lax.rem(value, CHIPS)
                    used = jnp.full((1, LANES), (value < CHIPS).astype(F32)).astype(BF16)
                    col = (k * CHIPS + n) * TILE
                    placed[:, col:col + TILE] = blocks[block] * used

    for tick in range(TICKS):
        if tick:
            base_done(tick)
        acc[...] = dot(weights[TOP], base_rows(tick))
        if tick:
            @pl.when(inner)
            def _():
                take_products(tick - 1)
        if tick == 1:
            @pl.when(s == 0)
            def _():
                pass_codes()
                pass_on(0)
        if tick < TICKS - 1:
            for k in range(2):
                own_products[tick, k] = acc[k * TILE:(k + 1) * TILE].astype(BF16)
            for node in ROOTS:
                for k in range(2):
                    root(tick, k, node).start()
        else:
            reduce_out(tick)
        if tick == 0:
            @pl.when(inner)
            def _():
                pass_codes()
        if tick == 0:
            sib_diag().wait_recv()
            for b in range(CHIPS):
                blocks[b] = weights[:, b * TILE:(b + 1) * TILE]
        sol_send[tick] = dot(weights[LOW], base_rows(tick))
        if tick:
            @pl.when(inner)
            def _():
                for k in range(2):
                    for part in range(2):
                        sol_send[tick] = sol_send[tick] - placed_dot(LOW, tick - 1, k, part)
                give_back(tick - 1)
        lanes = pl.ds(pl.multiple_of(tick * PW + core * LANES, LANES), LANES)
        sol_out[:, lanes] = sol_send[tick, my_rows]
        sib_sol(tick).start()
        if tick < TICKS - 1:
            @pl.when(inner)
            def _():
                pass_on(tick)
        if tick == 0:
            base_over(2, RING)
        if tick == 0:
            @pl.when(inner)
            def _():
                read_codes(True)

    @pl.when(s == 0)
    def _():
        read_codes(False)
        pl.semaphore_wait(last_in, 2)
        for tick in range(TICKS - 1):
            if tick:
                pass_on(tick)
            for k in range(2):
                for part in range(2):
                    parts_in(tick, k, part)
            give_back(tick)

    drain(back_recv, back_r)
    for tick in range(TICKS - 1):
        for k in range(2):
            upd_out[:, tick * PW + k * LANES:tick * PW + (k + 1) * LANES] = back_recv[tick, k]
    drain(sol_recv, sib_recv.at[6])
    for tick in range(TICKS):
        lanes = pl.ds(pl.multiple_of(tick * PW + (1 - core) * LANES, LANES), LANES)
        sol_out[:, lanes] = sol_recv[tick]
    reduce_in(TICKS - 1)
    drain(other_base, sib_send.at[0])
    drain(code_own, sib_send.at[1])
    drain(weights.at[:TILE], sib_send.at[2])
    drain(weights.at[:HALF], sib_send.at[3])
    drain(sol_recv, sib_send.at[4])
    drain(base.at[:, :n_far], base_s)
    drain(codes, code_s)
    drain(products, ring_s)
    drain(back_send, back_s)
    drain(block_recv.at[:2 * CHIPS - 1], red_s)


def body(*arrays):
    right_side = arrays[0]
    rows, width = right_side.shape
    dma = pltpu.SemaphoreType.DMA
    any_spec = pl.BlockSpec(memory_space=pl.ANY)
    hbm_spec = pl.BlockSpec(memory_space=pltpu.HBM)
    vmem = pl.BlockSpec(memory_space=pltpu.VMEM)
    out = pltpu.VMEM((2 * rows, width), F32)
    both = pl.pallas_call(
        kernel,
        out_shape=out,
        in_specs=[any_spec] * 5 + [hbm_spec] * 3,
        out_specs=vmem,
        scratch_shapes=[
            pltpu.SMEM(arrays[5].shape, jnp.int32),
            pltpu.SMEM(arrays[6].shape, jnp.int32),
            pltpu.SMEM(arrays[7].shape, jnp.int32),
            pltpu.SMEM((2 * CHIPS,), jnp.int32),
            pltpu.VMEM((rows, width), BF16),
            pltpu.VMEM((rows, PW), F32),
            pltpu.VMEM((rows, 2 * PW), F32),
            pltpu.VMEM((3 * TILE, W), BF16),
            pltpu.VMEM((CHIPS, 3 * TILE, LANES), BF16),
            pltpu.VMEM((3 * TILE, 2 * W), BF16),
            pltpu.VMEM((TICKS, CHIPS, TILE, LANES), BF16),
            pltpu.VMEM((TICKS, HALF, LANES), BF16),
            pltpu.VMEM((TICKS - 1, 2, CHIPS, TILE, LANES), BF16),
            pltpu.VMEM((TICKS - 1, 2, TILE, LANES), BF16),
            pltpu.VMEM((2 * TILE, LANES), F32),
            pltpu.VMEM((8, LANES), jnp.int32),
            pltpu.VMEM((8, LANES), jnp.int32),
            pltpu.VMEM((8, LANES), jnp.int32),
            pltpu.VMEM((CHIPS, 8, LANES), jnp.int32),
            pltpu.VMEM((TICKS, TILE, LANES), F32),
            pltpu.VMEM((TICKS, HALF, LANES), F32),
            pltpu.VMEM((TICKS - 1, TILE, LANES), F32),
            pltpu.VMEM((TICKS - 1, 2, HALF, LANES), F32),
            pltpu.VMEM((CHIPS, TILE, LANES), BF16),
            pltpu.VMEM((2 * CHIPS, HALF, LANES), BF16),
            dma((8,)), dma((5,)), dma((7,)),
            dma, dma((TICKS, 2)), dma, dma((2,)),
            dma, dma((2, 2, SIDE + 2)), dma, dma, dma, dma,
            pltpu.SemaphoreType.REGULAR,
        ],
        compiler_params=pltpu.CompilerParams(collective_id=0, has_side_effects=True),
        name="chain_solve",
    )(*arrays)
    return both[:rows], both[rows:]


def solution(mesh):
    placed = (
        P(("chain", "rows"), None),
        P(("chain", "rows"), None),
        P("rows", None),
        P("chain", "rows", None),
        P("chain", "rows", None, None),
        P("chain", "rows"),
        P("chain", None),
        P("chain"),
    )
    return jax.shard_map(
        body,
        mesh=mesh,
        in_specs=placed,
        out_specs=(P(("chain", "rows"), None), P(("chain", "rows"), None)),
        check_vma=False,
    )
```

```python
import jax
import jax.numpy as jnp
from jax import lax
from jax.experimental import pallas as pl
from jax.experimental.pallas import tpu as pltpu
from jax.sharding import PartitionSpec as P

PW = 256
TILE = 128
HALF = 64
W = 2048
NZ = 8
SIDE = 4
CHIPS = SIDE * SIDE
TICKS = 3
LANES = 128
F32 = jnp.float32
BF16 = jnp.bfloat16
MESH = pl.DeviceIdType.MESH
HOPS = (1, 3, 2)
RING = (0,) + HOPS
FAR_FIRST = tuple((a, b) for a in range(SIDE - 1, -1, -1) for b in range(SIDE - 1, -1, -1) if (a, b) != (0, 0))
NODES = tuple((f, e) for e in RING for f in range(SIDE))
ROOTS = ((0, 0), (1, 0), (3, 0), (2, 0))
EVENTS = tuple(((f, 0), tuple((f, e) for e in HOPS)) for f in RING)
CHUNK = 8


def slot(f, e):
    return NODES.index((f, e))


def kernel(
    right_side, entering, first_updates, diag_inverse, tile_blocks, targets_in, order_in, count_in,
    both_out,
    targets, order, count, code_table,
    given, enter, first, weights, blocks, placed, base, other_base, products, own_products, acc,
    code_own, code_sib, code_send, codes, sol_send, sol_recv, back_send, back_recv,
    block_send, block_recv,
    load_sem, sib_send, sib_recv, base_s, base_r, code_s, code_r,
    ring_s, ring_r, back_s, back_r, red_s, red_r, last_in,
):
    rows_out = both_out.shape[0] // 2
    sol_out, upd_out = both_out.at[:rows_out], both_out.at[rows_out:]
    s = lax.axis_index("chain")
    row = lax.axis_index("rows")
    core = lax.rem(row, 2)
    chip = row // 2
    x = lax.rem(chip, SIDE)
    y = chip // SIDE
    p1 = x + core * (y - x)
    p2 = y + core * (x - y)
    stride1 = 1 + 3 * core
    stride2 = 4 - 3 * core
    up = lax.rem(s + 1, NZ)
    down = lax.rem(s + NZ - 1, NZ)
    sibling = (s, row + 1 - 2 * core)

    def chip_at(d1, d2):
        return lax.rem(p1 + d1 + SIDE, SIDE) * stride1 + lax.rem(p2 + d2 + SIDE, SIDE) * stride2

    def at(plane, d1, d2):
        return (plane, chip_at(d1, d2) * 2 + core)

    def across(plane, d1, d2):
        return (plane, chip_at(d1, d2) * 2 + 1 - core)

    def remote(src, dst, ssem, rsem, device):
        return pltpu.make_async_remote_copy(
            src_ref=src, dst_ref=dst, send_sem=ssem, recv_sem=rsem,
            device_id=device, device_id_type=MESH,
        )

    def drain(ref, sem):
        pltpu.make_async_copy(ref, ref, sem).wait()

    barrier = pltpu.get_barrier_semaphore()

    def greet(device):
        pl.semaphore_signal(barrier, inc=1, device_id=device, device_id_type=MESH)

    greet(sibling)
    for a, b in FAR_FIRST:
        greet(at(s, a, b))
        greet(across(s, a, b))
    in_plane = 1 + 2 * len(FAR_FIRST)
    z_moves = [(f, 0) for f, _ in ROOTS] + [(0, f) for f, _ in ROOTS if f]
    in_z = len(z_moves) + 1
    for a, b in z_moves:
        greet(at(down, SIDE - a, SIDE - b))
    greet(across(down, 0, 0))

    @pl.when(s < NZ - 1)
    def _():
        for a, b in z_moves:
            greet(at(up, a, b))
        greet(across(up, 0, 0))

    my_rows = pl.ds(pl.multiple_of(core * HALF, HALF), HALF)
    their_rows = pl.ds(pl.multiple_of((1 - core) * HALF, HALF), HALF)
    tile_rows = pl.ds(pl.multiple_of(core * TILE, TILE), TILE)
    diag_rows = pl.ds(pl.multiple_of(2 * TILE + core * HALF, HALF), HALF)
    loads = [
        pltpu.make_async_copy(right_side, given, load_sem.at[0]),
        pltpu.make_async_copy(entering, enter, load_sem.at[1]),
        pltpu.make_async_copy(first_updates, first, load_sem.at[2]),
        pltpu.make_async_copy(targets_in, targets, load_sem.at[3]),
        pltpu.make_async_copy(order_in, order, load_sem.at[4]),
        pltpu.make_async_copy(count_in, count, load_sem.at[5]),
        pltpu.make_async_copy(tile_blocks.at[0, 0], weights.at[tile_rows], load_sem.at[6]),
        pltpu.make_async_copy(diag_inverse.at[0], weights.at[diag_rows], load_sem.at[7]),
    ]
    for copy in loads:
        copy.start()
    for copy in loads[:3]:
        copy.wait()
    is_first = (s == 0).astype(F32)

    def head_part(tick, half):
        lanes = pl.ds(pl.multiple_of(tick * PW + half * LANES, LANES), LANES)
        value = given[:, lanes].astype(F32)
        if tick == 0:
            taken = enter[:, pl.ds(pl.multiple_of(half * LANES, LANES), LANES)]
        else:
            lanes = pl.ds(pl.multiple_of((tick - 1) * PW + half * LANES, LANES), LANES)
            taken = is_first * first[:, lanes]
        return (value - taken).astype(BF16)

    for tick in range(TICKS):
        other_base[tick] = head_part(tick, 1 - core)
        base[tick, chip, my_rows] = head_part(tick, core)

    for copy in loads[3:6]:
        copy.wait()
    live = jnp.int32(0)
    for k in range(order.shape[1]):
        hit = jnp.logical_and(order[0, k] == row, k < count[0])
        live = live + hit.astype(jnp.int32)
    code = targets[0, 0] + CHIPS * (1 - live)
    code_rows = lax.broadcasted_iota(jnp.int32, (8, LANES), 0)
    code_own[...] = jnp.where(code_rows == core, code, 0)

    pl.semaphore_wait(barrier, in_plane + in_z + in_z * (s > 0).astype(jnp.int32))

    @pl.when(s == NZ - 1)
    def _():
        for device in (at(up, 0, 0), across(up, 0, 0)):
            pl.semaphore_signal(last_in, inc=1, device_id=device, device_id_type=MESH)

    def sib_base(tick):
        return remote(
            other_base.at[tick], base.at[tick, chip, my_rows],
            sib_send.at[0], sib_recv.at[tick], sibling,
        )

    def sib_code():
        return remote(code_own, code_sib, sib_send.at[1], sib_recv.at[3], sibling)

    def sib_tile():
        return remote(tile_blocks.at[0, 0], weights.at[tile_rows], sib_send.at[2], sib_recv.at[4], sibling)

    def sib_diag():
        return remote(diag_inverse.at[0], weights.at[diag_rows], sib_send.at[3], sib_recv.at[5], sibling)

    def base_half(rows, d1, d2):
        return remote(
            base.at[0, chip, rows], base.at[0, chip, rows],
            base_s, base_r.at[0, 0], at(s, d1, d2),
        )

    n_far = len(FAR_FIRST)
    def base_copy(tick, node, child):
        held = chip_at(-node[0], -node[1])
        return remote(
            base.at[tick, held], base.at[tick, held], base_s, base_r.at[tick, int(child[1] > 0)],
            at(s, child[0] - node[0], child[1] - node[1]),
        )

    def base_along(tick):
        sib_base(tick).wait_recv()
        for f in (3, 1, 2):
            base_copy(tick, (0, 0), (f, 0)).start()

    def base_over(tick, rings=RING):
        if rings[0] == 0:
            drain(base.at[tick, :SIDE - 1], base_r.at[tick, 0])
        for f in rings:
            for e in (3, 1, 2):
                base_copy(tick, (f, 0), (f, e)).start()

    def base_done(tick):
        drain(base.at[tick, :CHIPS - SIDE], base_r.at[tick, 1])

    sib_base(0).start()
    sib_base(1).start()
    sib_code().start()
    for a, b in FAR_FIRST:
        base_half(my_rows, a, b).start()
    sib_base(0).wait_recv()
    sib_base(1).wait_recv()
    for f in HOPS:
        base_copy(1, (0, 0), (f, 0)).start()
    for a, b in FAR_FIRST:
        base_half(their_rows, b, a).start()
    sib_base(2).start()

    def code_root(f, e):
        return remote(code_send, codes.at[slot(f, e)], code_s, code_r.at[0], at(up, f, e))

    def code_edge(node, child):
        n, m = slot(*node), slot(*child)
        return remote(
            codes.at[n], codes.at[m], code_s, code_r.at[1],
            at(s, child[0] - node[0], child[1] - node[1]),
        )

    sib_code().wait_recv()
    code_send[...] = code_own[...] + code_sib[...]

    for f, e in ROOTS:
        code_root(f, e).start()

    sib_tile().start()
    sib_diag().start()

    base_along(2)
    for copy in loads[6:]:
        copy.wait()
    sib_tile().wait_recv()
    sib_diag().wait_recv()
    for b in range(CHIPS):
        blocks[b] = weights[:, b * TILE:(b + 1) * TILE]

    def pass_codes():
        drain(codes.at[:SIDE], code_r.at[0])
        for node, children in EVENTS:
            for child in children:
                code_edge(node, child).start()


    base_over(1, RING)
    drain(base.at[0, :n_far], base_r.at[0, 0])

    def dot(a, b):
        return jnp.dot(a, b, preferred_element_type=F32)

    def base_rows(tick):
        return base[tick].reshape(W, LANES)

    TOP = slice(0, 2 * TILE)
    LOW = slice(2 * TILE, 3 * TILE)
    def placed_dot(rows, tick, k, part):
        first_slot = part * CHUNK
        col = (k * CHIPS + first_slot) * TILE
        right = products[tick, k, first_slot:first_slot + CHUNK].reshape(CHUNK * TILE, LANES)
        return dot(placed[rows, col:col + CHUNK * TILE], right)

    def move(k, f, e):
        return (f, e) if k == 0 else (e, f)

    def root(tick, k, node):
        n = slot(*node)
        return remote(
            own_products.at[tick, k], products.at[tick, k, n],
            ring_s, ring_r.at[tick, k, n], at(up, *move(k, *node)),
        )

    def edge(tick, k, node, child):
        n, m = slot(*node), slot(*child)
        return remote(
            products.at[tick, k, n], products.at[tick, k, m],
            ring_s, ring_r.at[tick, k, m if m < SIDE else SIDE + m // CHUNK],
            at(s, *move(k, child[0] - node[0], child[1] - node[1])),
        )

    def parts_in(tick, k, part):
        drain(products.at[tick, k, max(part * CHUNK, SIDE):(part + 1) * CHUNK], ring_r.at[tick, k, SIDE + part])

    def pass_on(tick):
        for j, (node, children) in enumerate(EVENTS):
            for k in range(2):
                drain(products.at[tick, k, slot(*node)], ring_r.at[tick, k, slot(*node)])
                for child in children:
                    edge(tick, k, node, child).start()

    def take_products(tick):
        for part in range(2):
            for k in range(2):
                parts_in(tick, k, part)
                acc[...] = acc[...] - placed_dot(TOP, tick, k, part)

    def give_back(tick):
        total = jnp.zeros((TILE, LANES), F32)
        for k in range(2):
            for n in range(CHIPS):
                part = products[tick, k, n].astype(F32)
                total = total + (code_table[k * CHIPS + n] == chip).astype(F32) * part
        back_send[tick] = total
        for h in range(2):
            back(tick, h, core).start()

    def back(tick, h, k):
        return remote(
            back_send.at[tick, h * HALF:(h + 1) * HALF], back_recv.at[tick, k],
            back_s, back_r, (down, chip * 2 + h),
        )

    code_both = [jnp.max(code_send[k:k + 1, :]) for k in range(2)]

    def own_half(n, a, b):
        return remote(
            block_send.at[n, my_rows], block_recv.at[core * CHIPS + n],
            red_s, red_r, at(s, a, b),
        )

    def other_half(n, a, b):
        return remote(
            block_send.at[n, their_rows], block_recv.at[core * CHIPS + n],
            red_s, red_r, across(s, a, b),
        )

    def reduce_out(tick):
        def reduced(target):
            m0 = (code_both[0] == target).astype(F32)
            m1 = (code_both[1] == target).astype(F32)
            return (m0 * acc[:TILE] + m1 * acc[TILE:]).astype(BF16)

        for n, (a, b) in enumerate(FAR_FIRST):
            block_send[n] = reduced(chip_at(a, b))
            own_half(n, a, b).start()
        block_send[n_far] = reduced(chip)
        other_half(n_far, 0, 0).start()
        for b, a in FAR_FIRST:
            n = FAR_FIRST.index((a, b))
            other_half(n, a, b).start()
        block_recv[core * CHIPS + n_far] = block_send[n_far, my_rows]

    def reduce_in(tick):
        drain(block_recv.at[:2 * CHIPS - 1], red_r)
        for k in range(2):
            total = jnp.zeros((HALF, LANES), F32)
            for n in range(CHIPS):
                total = total + block_recv[k * CHIPS + n].astype(F32)
            upd_out[:, tick * PW + k * LANES:tick * PW + (k + 1) * LANES] = total

    def sib_sol(tick):
        return remote(
            sol_send.at[tick, their_rows], sol_recv.at[tick],
            sib_send.at[4], sib_recv.at[6], sibling,
        )

    inner = s > 0

    def read_codes(place):
        drain(codes.at[SIDE:], code_r.at[1])
        for k in range(2):
            for n, (f, e) in enumerate(NODES):
                value = jnp.max(codes[slot(*move(k, f, e)), k:k + 1, :])
                code_table[k * CHIPS + n] = value
                if place:
                    block = lax.rem(value, CHIPS)
                    used = jnp.full((1, LANES), (value < CHIPS).astype(F32)).astype(BF16)
                    col = (k * CHIPS + n) * TILE
                    placed[:, col:col + TILE] = blocks[block] * used

    for tick in range(TICKS):
        if tick:
            base_done(tick)
        acc[...] = dot(weights[TOP], base_rows(tick))
        if tick:
            @pl.when(inner)
            def _():
                take_products(tick - 1)
        if tick == 1:
            @pl.when(s == 0)
            def _():
                pass_codes()
                pass_on(0)
        if tick < TICKS - 1:
            for k in range(2):
                own_products[tick, k] = acc[k * TILE:(k + 1) * TILE].astype(BF16)
            for node in ROOTS:
                for k in range(2):
                    root(tick, k, node).start()
        else:
            reduce_out(tick)
        if tick == 0:
            @pl.when(inner)
            def _():
                pass_codes()
        sol_send[tick] = dot(weights[LOW], base_rows(tick))
        if tick:
            @pl.when(inner)
            def _():
                for k in range(2):
                    for part in range(2):
                        sol_send[tick] = sol_send[tick] - placed_dot(LOW, tick - 1, k, part)
                give_back(tick - 1)
        lanes = pl.ds(pl.multiple_of(tick * PW + core * LANES, LANES), LANES)
        sol_out[:, lanes] = sol_send[tick, my_rows]
        sib_sol(tick).start()
        if tick < TICKS - 1:
            @pl.when(inner)
            def _():
                pass_on(tick)
        if tick == 0:
            base_over(2, RING)
        if tick == 0:
            @pl.when(inner)
            def _():
                read_codes(True)

    @pl.when(s == 0)
    def _():
        read_codes(False)
        pl.semaphore_wait(last_in, 2)
        for tick in range(TICKS - 1):
            if tick:
                pass_on(tick)
            for k in range(2):
                for part in range(2):
                    parts_in(tick, k, part)
            give_back(tick)

    drain(back_recv, back_r)
    for tick in range(TICKS - 1):
        for k in range(2):
            upd_out[:, tick * PW + k * LANES:tick * PW + (k + 1) * LANES] = back_recv[tick, k]
    drain(sol_recv, sib_recv.at[6])
    for tick in range(TICKS):
        lanes = pl.ds(pl.multiple_of(tick * PW + (1 - core) * LANES, LANES), LANES)
        sol_out[:, lanes] = sol_recv[tick]
    reduce_in(TICKS - 1)
    drain(other_base, sib_send.at[0])
    drain(code_own, sib_send.at[1])
    drain(weights.at[:TILE], sib_send.at[2])
    drain(weights.at[:HALF], sib_send.at[3])
    drain(sol_recv, sib_send.at[4])
    drain(base.at[:, :n_far], base_s)
    drain(codes, code_s)
    drain(products, ring_s)
    drain(back_send, back_s)
    drain(block_recv.at[:2 * CHIPS - 1], red_s)


def body(*arrays):
    right_side = arrays[0]
    rows, width = right_side.shape
    dma = pltpu.SemaphoreType.DMA
    any_spec = pl.BlockSpec(memory_space=pl.ANY)
    hbm_spec = pl.BlockSpec(memory_space=pltpu.HBM)
    vmem = pl.BlockSpec(memory_space=pltpu.VMEM)
    out = pltpu.VMEM((2 * rows, width), F32)
    both = pl.pallas_call(
        kernel,
        out_shape=out,
        in_specs=[any_spec] * 5 + [hbm_spec] * 3,
        out_specs=vmem,
        scratch_shapes=[
            pltpu.SMEM(arrays[5].shape, jnp.int32),
            pltpu.SMEM(arrays[6].shape, jnp.int32),
            pltpu.SMEM(arrays[7].shape, jnp.int32),
            pltpu.SMEM((2 * CHIPS,), jnp.int32),
            pltpu.VMEM((rows, width), BF16),
            pltpu.VMEM((rows, PW), F32),
            pltpu.VMEM((rows, 2 * PW), F32),
            pltpu.VMEM((3 * TILE, W), BF16),
            pltpu.VMEM((CHIPS, 3 * TILE, LANES), BF16),
            pltpu.VMEM((3 * TILE, 2 * W), BF16),
            pltpu.VMEM((TICKS, CHIPS, TILE, LANES), BF16),
            pltpu.VMEM((TICKS, HALF, LANES), BF16),
            pltpu.VMEM((TICKS - 1, 2, CHIPS, TILE, LANES), BF16),
            pltpu.VMEM((TICKS - 1, 2, TILE, LANES), BF16),
            pltpu.VMEM((2 * TILE, LANES), F32),
            pltpu.VMEM((8, LANES), jnp.int32),
            pltpu.VMEM((8, LANES), jnp.int32),
            pltpu.VMEM((8, LANES), jnp.int32),
            pltpu.VMEM((CHIPS, 8, LANES), jnp.int32),
            pltpu.VMEM((TICKS, TILE, LANES), F32),
            pltpu.VMEM((TICKS, HALF, LANES), F32),
            pltpu.VMEM((TICKS - 1, TILE, LANES), F32),
            pltpu.VMEM((TICKS - 1, 2, HALF, LANES), F32),
            pltpu.VMEM((CHIPS, TILE, LANES), BF16),
            pltpu.VMEM((2 * CHIPS, HALF, LANES), BF16),
            dma((8,)), dma((5,)), dma((7,)),
            dma, dma((TICKS, 2)), dma, dma((2,)),
            dma, dma((2, 2, SIDE + 2)), dma, dma, dma, dma,
            pltpu.SemaphoreType.REGULAR,
        ],
        compiler_params=pltpu.CompilerParams(collective_id=0, has_side_effects=True),
        name="chain_solve",
    )(*arrays)
    return both[:rows], both[rows:]


def solution(mesh):
    placed = (
        P(("chain", "rows"), None),
        P(("chain", "rows"), None),
        P("rows", None),
        P("chain", "rows", None),
        P("chain", "rows", None, None),
        P("chain", "rows"),
        P("chain", None),
        P("chain"),
    )
    return jax.shard_map(
        body,
        mesh=mesh,
        in_specs=placed,
        out_specs=(P(("chain", "rows"), None), P(("chain", "rows"), None)),
        check_vma=False,
    )
```
